512 devices in a mesh: wide: 128 (over x, y, z_lo, core), narrow: 4 (over z_hi).
Axes of the slice: x: 4, y: 4, z: 16 (z_hi: 4, z_lo: 4; z = z_hi * 4 + z_lo), core: 2. Of those that a mesh axis runs over, the one named last changes fastest.
Arguments:
- corr_panel: float32 [65536, 512], P('wide', 'narrow'), may hold values from -24 to 24
- factor_prev: float32 [65536, 1024], P('wide', 'narrow'), may hold values from -400 to 400
- draws_prev: float32 [1024, 512], P('narrow'), may hold values from -6 to 6
- draws_panel: float32 [512, 512], P('narrow'), may hold values from -6 to 6
- diag_inverse: float32 [512, 512], P('narrow'), may hold values from -1 to 1, as said below
Outputs:
- panel_factor: float32 [65536, 512], P('wide', 'narrow')
- smoothed: float32 [512, 65536], P(('narrow', 'wide'))
The draws below stay inside these ranges and needn't reach their ends.
Inputs may be any that keep to these rules, and one draw needn't show every extreme that they name: `diag_inverse`: lower triangular with a positive diagonal.
All inputs are finite; a program needn't handle non-finite values.
Results may differ from the reference program's by a relative error of at most 0.0003.
Values sent between devices are 32-bit elements; how exact they have to be, the bound alone decides.
A program may use at most 64 MiB of HBM per device.

```python
import math
import jax
import jax.numpy as jnp
from jax import lax

PANEL = 512
WIN = 5
N = 65536
K = 1024
S = 512


def draw_factor_prev(key, part):
    row_key, col_key, value_key = jax.random.split(key, 3)
    col_ramp = jnp.arange(K, dtype=jnp.float32) / K
    row_scale = jnp.exp(jax.random.uniform(row_key, (N, 1), jnp.float32) * math.log(10.0))
    col_scale = jnp.exp(col_ramp * math.log(3.0) + jax.random.uniform(col_key, (K,), jnp.float32) * math.log(2.0))
    values = jax.random.truncated_normal(value_key, -5.0, 5.0, (N, K), jnp.float32)
    return values * row_scale * col_scale[None, :] * K ** (-0.25)


def draw_diag_inverse(key, part):
    off_key, diag_key = jax.random.split(key)
    off_values = jax.random.truncated_normal(off_key, -5.0, 5.0, (PANEL, PANEL), jnp.float32)
    diag_values = jax.random.uniform(diag_key, (PANEL,), jnp.float32, 0.05, 0.15)
    lower_part = jnp.tril(off_values, -1) * (0.1 / math.sqrt(PANEL))
    return lower_part + jnp.diag(diag_values)


def levels(own_key, shape, cuts, smallest, high):
    loudness, own = 1.0, jax.random.fold_in(own_key, 6)
    for axis_at, parts in cuts:
        steps = jnp.exp(jax.random.uniform(jax.random.fold_in(own, axis_at), (parts,), jnp.float32, smallest / len(cuts), high / len(cuts)))
        loudness = loudness * jnp.repeat(steps, shape[axis_at] // parts).reshape([-1 if axis == axis_at else 1 for axis in range(len(shape))])
    return loudness


def scatter_about(rng, extent, scale, most, pieces=(), kind=jnp.bfloat16):
    gain = levels(rng, extent, pieces, -0.22, 0.18) if pieces else 1.0
    entries = jax.random.normal(rng, extent, jnp.float32) * scale * gain
    return jnp.minimum(jnp.maximum(entries, -most), most).astype(kind)


def setup_inputs(seed: int = 0) -> dict:
    key_of = jax.random.split(jax.random.key(seed), 6)
    corr_panel = scatter_about(key_of[0], (N, PANEL), 4.0, 24.0, ((0, 128), (1, 4)), jnp.float32)
    factor_prev = draw_factor_prev(jax.random.fold_in(key_of[5], 71), 0)
    draws_prev = scatter_about(key_of[2], (K, S), 1.0, 6.0, ((0, 4),), jnp.float32)
    draws_panel = scatter_about(key_of[3], (PANEL, S), 1.0, 6.0, ((0, 4),), jnp.float32)
    diag_inverse = draw_diag_inverse(jax.random.fold_in(key_of[5], 71), 0)
    return {"corr_panel": corr_panel, "factor_prev": factor_prev, "draws_prev": draws_prev, "draws_panel": draws_panel, "diag_inverse": diag_inverse}


def smooth(uniforms):
    half_span = (WIN - 1) // 2
    feature_count = uniforms.shape[1]
    padded = jnp.pad(uniforms, ((0, 0), (half_span, half_span)))
    summed = jnp.zeros_like(uniforms)
    for offset in range(WIN):
        weight_tap = math.comb(WIN - 1, offset) / 2.0 ** (WIN - 1)
        summed = summed + weight_tap * padded[:, offset:offset + feature_count]
    return summed

def reference(corr_panel, factor_prev, draws_prev, draws_panel, diag_inverse):
    exact_mode = lax.Precision.HIGHEST
    pivot_block = factor_prev[K:K + PANEL, :]
    updated = corr_panel - jnp.dot(factor_prev, pivot_block.T, precision=exact_mode, preferred_element_type=jnp.float32)
    panel_factor = jnp.dot(updated, diag_inverse.T, precision=exact_mode, preferred_element_type=jnp.float32)
    samples = jnp.dot(draws_prev.T, factor_prev.T, precision=exact_mode, preferred_element_type=jnp.float32)
    samples = samples + jnp.dot(draws_panel.T, panel_factor.T, precision=exact_mode, preferred_element_type=jnp.float32)
    variance = lax.optimization_barrier(jnp.sum(factor_prev * factor_prev, axis=1)) + lax.optimization_barrier(jnp.sum(panel_factor * panel_factor, axis=1))
    scaled = samples * lax.rsqrt(variance + 1e-06)[None, :]
    uniforms = 0.5 * (1.0 + lax.erf(scaled * (1.0 / math.sqrt(2.0))))
    return (panel_factor, smooth(uniforms))
```

```python
import functools
import math

import jax
import jax.numpy as jnp
from jax import lax
from jax.experimental import pallas as pl
from jax.experimental.pallas import tpu as pltpu
from jax.sharding import PartitionSpec as P

MESH = pl.DeviceIdType.MESH
EXACT = lax.Precision.HIGHEST
HALF_ROOT = 1.0 / math.sqrt(2.0)
X, Y, Z, CORES = 4, 4, 4, 2
WIDE = X * Y * Z * CORES
NARROW = 4
OWNER = 2
PLANE = X * Y * CORES


def wide_of(x, y, z, core):
    return ((x * Y + y) * Z + z) * CORES + core


def rem4(value):
    return lax.rem(value, 4)


def dot(left, right, left_dim, right_dim):
    return lax.dot_general(
        left,
        right,
        (((left_dim,), (right_dim,)), ((), ())),
        precision=EXACT,
        preferred_element_type=jnp.float32,
    )


def kernel(
    corr,
    factor,
    draws_prev,
    draws_panel,
    inverse,
    panel_out,
    smooth_out,
    f_rows,
    c_rows,
    d1,
    dv,
    piv,
    updated,
    panel,
    uni,
    mixed,
    full,
    own_sem,
    d_send,
    d_recv,
    p1_send,
    p1_recv,
    p2_send,
    p2_recv,
    f_send,
    f_recv,
    g1_send,
    g1_recv,
    g2_send,
    g2_recv,
    x_send,
    x_recv,
    q_send,
    q_recv,
    u_send,
    u_recv,
    a_send,
    a_recv,
):
    wide = lax.axis_index("wide")
    n = lax.axis_index("narrow")
    core = lax.rem(wide, CORES)
    z = rem4(lax.div(wide, CORES))
    y = rem4(lax.div(wide, CORES * Z))
    x = lax.div(wide, CORES * Z * Y)
    a = core * x + (1 - core) * y
    b = core * y + (1 - core) * x
    place = 16 * core + 4 * a + b

    def send(src, dst, send_sem, recv_sem, to_wide, to_narrow):
        copy = pltpu.make_async_remote_copy(
            src_ref=src,
            dst_ref=dst,
            send_sem=send_sem,
            recv_sem=recv_sem,
            device_id={"wide": to_wide, "narrow": to_narrow},
            device_id_type=MESH,
        )
        copy.start()
        return copy

    barrier = pltpu.get_barrier_semaphore()

    def greet(step, carry):
        pl.semaphore_signal(
            barrier,
            inc=1,
            device_id={"wide": lax.rem(wide + step, WIDE), "narrow": n},
            device_id_type=MESH,
        )
        return carry

    lax.fori_loop(1, WIDE, greet, 0)
    for k in range(1, NARROW):
        for z_other in range(Z):
            pl.semaphore_signal(
                barrier,
                inc=1,
                device_id={"wide": wide_of(x, y, z_other, core), "narrow": rem4(n + k)},
                device_id_type=MESH,
            )

    own = [
        pltpu.make_async_copy(draws_prev, d1.at[0], own_sem.at[0]),
        pltpu.make_async_copy(draws_panel, dv.at[0, 0], own_sem.at[1]),
        pltpu.make_async_copy(inverse, dv.at[1, 0], own_sem.at[2]),
        pltpu.make_async_copy(factor.at[pl.ds(128 * n, 128)], f_rows.at[0], own_sem.at[3]),
        pltpu.make_async_copy(corr.at[pl.ds(128 * n, 128)], c_rows.at[n], own_sem.at[4]),
    ]
    for copy in own:
        copy.start()
    for copy in own:
        copy.wait()
    pl.semaphore_wait(barrier, WIDE - 1 + (NARROW - 1) * Z)

    rows8 = pl.ds(8 * place, 8)
    rows8_core = pl.ds(8 * (4 * a + b), 8)
    rows16 = pl.ds(16 * place, 16)
    d_copies = []
    for k in range(1, NARROW):
        peer = rem4(n + k)
        d_copies.append(
            send(d1.at[0, rows8], d1.at[4 - k, rows8], d_send.at[k - 1, 0], d_recv.at[k - 1, 0], wide, peer)
        )
        d_copies.append(
            send(
                dv.at[core, 0, rows8_core],
                dv.at[core, 4 - k, rows8_core],
                d_send.at[k - 1, 1],
                d_recv.at[k - 1, 1],
                wide,
                peer,
            )
        )

    @pl.when(wide == OWNER)
    def _():
        copies = []
        for to in range(1, PLANE):
            to_core, to_a, to_b = to // 16, (to // 4) % 4, to % 4
            to_x, to_y = (to_a, to_b) if to_core else (to_b, to_a)
            rows = pl.ds(16 * to, 16)
            copies.append(
                send(
                    factor.at[rows],
                    piv.at[0, rows],
                    p1_send.at[to],
                    p1_recv,
                    wide_of(to_x, to_y, 1, to_core),
                    n,
                )
            )
        local = pltpu.make_async_copy(factor.at[pl.ds(0, 16)], piv.at[0, pl.ds(0, 16)], p1_send.at[0])
        local.start()
        local.wait()
        for copy in copies:
            copy.wait_send()

    @pl.when((z == 1) & (wide != OWNER))
    def _():
        pltpu.make_async_copy(piv.at[0, rows16], piv.at[0, rows16], p1_recv).wait()

    @pl.when(z == 1)
    def _():
        copies = []
        for k in range(NARROW):
            slot = rem4(4 - k)
            for z_other in range(Z):
                if k == 0 and z_other == 1:
                    continue
                copies.append(
                    send(
                        piv.at[0, rows16],
                        piv.at[(4 - k) % 4, rows16],
                        p2_send.at[k, z_other],
                        p2_recv.at[(4 - k) % 4],
                        wide_of(x, y, z_other, core),
                        rem4(n + k),
                    )
                )
        for copy in copies:
            copy.wait_send()

    f_copies = []
    for k in (2, 1, 3):
        peer = rem4(n + k)
        rows = pl.ds(128 * peer, 128)
        f_copies.append(
            (
                send(factor.at[rows], f_rows.at[4 - k], f_send.at[k - 1, 0], f_recv.at[k - 1, 0], wide, peer),
                send(corr.at[rows], c_rows.at[n], f_send.at[k - 1, 1], f_recv.at[k - 1, 1], wide, peer),
            )
        )

    for copy in d_copies:
        copy.wait()
    for slot in range(1, NARROW):
        pltpu.make_async_copy(piv.at[slot, rows16], piv.at[slot, rows16], p2_recv.at[slot]).wait()

    @pl.when(z != 1)
    def _():
        pltpu.make_async_copy(piv.at[0, rows16], piv.at[0, rows16], p2_recv.at[0]).wait()

    def pieces(first, count, at_core):
        in_core = first - 16 * at_core
        return (
            d1.at[pl.ds(1, 3), pl.ds(8 * first, 8 * count)],
            dv.at[at_core, pl.ds(1, 3), pl.ds(8 * in_core, 8 * count)],
            piv.at[:, pl.ds(16 * first, 16 * count)],
        )

    def along(step, use_y):
        return wide_of(rem4(x + step * (1 - use_y)), rem4(y + step * use_y), z, core)

    first_copies = []
    for step in (1, 3, 2):
        for kind, ref in enumerate(pieces(place, 1, core)):
            first_copies.append(
                send(ref, ref, g1_send.at[step - 1, kind], g1_recv.at[step - 1, kind], along(step, core), n)
            )
    for copy in first_copies:
        copy.wait()

    partner = wide_of(x, y, z, 1 - core)

    def to_partner(group, index):
        copies = []
        for kind, ref in enumerate(pieces(16 * core + 4 * group, 4, core)):
            copies.append(send(ref, ref, x_send.at[index, kind], x_recv.at[index, kind], partner, n))
        return copies

    second_copies = []
    for step in (1, 3, 2):
        for kind, ref in enumerate(pieces(16 * core + 4 * a, 4, core)):
            second_copies.append(
                send(ref, ref, g2_send.at[step - 1, kind], g2_recv.at[step - 1, kind], along(step, 1 - core), n)
            )
    core_copies = to_partner(a, 0)
    for order, step in enumerate((1, 3, 2)):
        for kind in range(3):
            second_copies[3 * order + kind].wait_recv()
        core_copies += to_partner(rem4(a + 4 - step), step)
    for copy in second_copies:
        copy.wait_send()
    for copy in core_copies:
        copy.wait()

    for pair in f_copies:
        for copy in pair:
            copy.wait()

    product = jnp.zeros((128, 512), jnp.float32)
    for k in range(NARROW):
        product = product + dot(f_rows[k], piv[k], 1, 1)
    for m in range(NARROW):
        updated[:, 128 * m : 128 * m + 128] = c_rows[m] - product[:, 128 * m : 128 * m + 128]
    squares = jnp.zeros((128, 1), jnp.float32)
    new = updated[...]
    for k in range(NARROW):
        value = dot(new, dv[1, k], 1, 1)
        panel[k] = value
        squares = squares + jnp.sum(value * value, axis=1, keepdims=True)
    q_copies = []
    for k in (2, 1, 3):
        q_copies.append(
            send(
                panel.at[k],
                panel_out.at[pl.ds(128 * n, 128)],
                q_send.at[k - 1],
                q_recv.at[k - 1],
                wide,
                rem4(n + k),
            )
        )
    panel_out[pl.ds(pl.multiple_of(128 * n, 128), 128), :] = panel[0]

    sums = jnp.zeros((128, 512), jnp.float32)
    for k in range(NARROW):
        part = f_rows[k]
        squares = squares + jnp.sum(part * part, axis=1, keepdims=True)
        sums = sums + dot(part, d1[k], 1, 0) + dot(panel[k], dv[0, k], 1, 0)
    scaled = sums * lax.rsqrt(squares + 1e-06)
    uniforms = 0.5 * (1.0 + lax.erf(scaled * HALF_ROOT))
    for m in range(NARROW):
        uni[m] = uniforms[:, 128 * m : 128 * m + 128].T.reshape(128, 1, 128)

    u_copies = []
    for k in (2, 1, 3):
        peer = rem4(n + k)
        u_copies.append(send(uni.at[peer], mixed.at[:, n], u_send.at[k - 1], u_recv.at[k - 1], wide, peer))
    local = pltpu.make_async_copy(uni.at[n], mixed.at[:, n], own_sem.at[0])
    local.start()
    local.wait()
    for copy in u_copies:
        copy.wait()

    mine = pl.ds(4 + 4 * wide, 4)

    def hand_out(step, carry):
        to = lax.rem(wide + step, WIDE)
        pltpu.make_async_remote_copy(
            src_ref=mixed.at[to],
            dst_ref=full.at[mine],
            send_sem=a_send,
            recv_sem=a_recv,
            device_id={"wide": to, "narrow": n},
            device_id_type=MESH,
        ).start()
        return carry

    lax.fori_loop(1, WIDE, hand_out, 0)
    local = pltpu.make_async_copy(mixed.at[wide], full.at[mine], own_sem.at[1])
    local.start()
    full[3] = jnp.zeros((1, 128), jnp.float32)
    full[516] = jnp.zeros((1, 128), jnp.float32)
    local.wait()
    for copy in q_copies:
        copy.wait()
    all_rows = pl.ds(4, 4 * (WIDE - 1))
    pltpu.make_async_copy(full.at[all_rows], full.at[all_rows], a_recv).wait()
    pltpu.make_async_copy(full.at[all_rows], full.at[all_rows], a_send).wait()

    before = full[3:515].reshape(512, 128)
    now = full[4:516].reshape(512, 128)
    after = full[5:517].reshape(512, 128)
    lane = lax.broadcasted_iota(jnp.int32, (512, 128), 1)
    total = 6.0 / 16.0 * now
    for shift, weight in ((1, 4.0 / 16.0), (2, 1.0 / 16.0)):
        left = jnp.where(lane < shift, pltpu.roll(before, shift, 1), pltpu.roll(now, shift, 1))
        right = jnp.where(lane >= 128 - shift, pltpu.roll(after, 128 - shift, 1), pltpu.roll(now, 128 - shift, 1))
        total = total + weight * (left + right)
    smooth_out[...] = total


def per_device(corr_panel, factor_prev, draws_prev, draws_panel, diag_inverse):
    anywhere = pl.BlockSpec(memory_space=pl.ANY)
    vmem = pl.BlockSpec(memory_space=pltpu.VMEM)
    dma = pltpu.SemaphoreType.DMA
    panel_factor, smoothed = pl.pallas_call(
        kernel,
        name="panel",
        out_shape=(
            jax.ShapeDtypeStruct((512, 128), jnp.float32),
            jax.ShapeDtypeStruct((512, 128), jnp.float32),
        ),
        in_specs=[anywhere] * 5,
        out_specs=(vmem, vmem),
        scratch_shapes=[
            pltpu.VMEM((4, 128, 256), jnp.float32),
            pltpu.VMEM((4, 128, 128), jnp.float32),
            pltpu.VMEM((4, 256, 512), jnp.float32),
            pltpu.VMEM((2, 4, 128, 512), jnp.float32),
            pltpu.VMEM((4, 512, 256), jnp.float32),
            pltpu.VMEM((128, 512), jnp.float32),
            pltpu.VMEM((4, 128, 128), jnp.float32),
            pltpu.VMEM((4, 128, 1, 128), jnp.float32),
            pltpu.VMEM((128, 4, 1, 128), jnp.float32),
            pltpu.VMEM((520, 1, 128), jnp.float32),
            dma((5,)),
            dma((3, 2)),
            dma((3, 2)),
            dma((PLANE,)),
            dma,
            dma((4, 4)),
            dma((4,)),
            dma((3, 2)),
            dma((3, 2)),
            dma((3, 3)),
            dma((3, 3)),
            dma((3, 3)),
            dma((3, 3)),
            dma((4, 3)),
            dma((4, 3)),
            dma((3,)),
            dma((3,)),
            dma((3,)),
            dma((3,)),
            dma,
            dma,
        ],
        compiler_params=pltpu.CompilerParams(
            collective_id=0, has_side_effects=True, vmem_limit_bytes=48 * 2**20
        ),
    )(corr_panel, factor_prev, draws_prev, draws_panel, diag_inverse)
    return panel_factor, smoothed.reshape(1, 512 * 128)


def solution(mesh):
    in_specs = (
        P("wide", "narrow"),
        P("wide", "narrow"),
        P("narrow", None),
        P("narrow", None),
        P("narrow", None),
    )
    out_specs = (P("wide", "narrow"), P(("narrow", "wide"), None))
    return jax.shard_map(
        per_device, mesh=mesh, in_specs=in_specs, out_specs=out_specs, check_vma=False
    )
```

```python
import functools
import math

import jax
import jax.numpy as jnp
from jax import lax
from jax.experimental import pallas as pl
from jax.experimental.pallas import tpu as pltpu
from jax.sharding import PartitionSpec as P

MESH = pl.DeviceIdType.MESH
HALF_ROOT = 1.0 / math.sqrt(2.0)
X, Y, Z, CORES = 4, 4, 4, 2
WIDE = X * Y * Z * CORES
NARROW = 4
OWNER = 2
PLANE = X * Y * CORES


def wide_of(x, y, z, core):
    return ((x * Y + y) * Z + z) * CORES + core


def rem4(value):
    return lax.rem(value, 4)


def dot(left, right, left_dim, right_dim):
    return lax.dot_general(
        left,
        right,
        (((left_dim,), (right_dim,)), ((), ())),
        preferred_element_type=jnp.float32,
    )


def split(value):
    head = value.astype(jnp.bfloat16)
    return head, (value - head.astype(jnp.float32)).astype(jnp.bfloat16)


def dot3(left, right, left_dim, right_dim):
    return dot(left[0], right[0], left_dim, right_dim) + (
        dot(left[0], right[1], left_dim, right_dim) + dot(left[1], right[0], left_dim, right_dim)
    )


def kernel(
    corr,
    factor,
    draws_prev,
    draws_panel,
    inverse,
    panel_out,
    smooth_out,
    f_rows,
    c_rows,
    d1,
    dv,
    piv,
    d1_split,
    dv_split,
    piv_split,
    updated,
    panel,
    uni,
    mixed,
    full,
    own_sem,
    d_send,
    d_recv,
    p1_send,
    p1_recv,
    p2_send,
    p2_recv,
    f_send,
    f_recv,
    g1_send,
    g1_recv,
    g2_send,
    g2_recv,
    x_send,
    x_recv,
    q_send,
    q_recv,
    u_send,
    u_recv,
    a_send,
    a_recv,
):
    wide = lax.axis_index("wide")
    n = lax.axis_index("narrow")
    core = lax.rem(wide, CORES)
    z = rem4(lax.div(wide, CORES))
    y = rem4(lax.div(wide, CORES * Z))
    x = lax.div(wide, CORES * Z * Y)
    a = core * x + (1 - core) * y
    b = core * y + (1 - core) * x
    place = 16 * core + 4 * a + b
    column = x * Y + y
    flat = column * CORES + core
    height = n * Z + z

    def in_plane(step):
        to = lax.rem(flat + step, PLANE)
        to_column, to_core = lax.div(to, CORES), lax.rem(to, CORES)
        return to, to_column, to_core, (to_column * Z + z) * CORES + to_core

    def in_ring(step):
        to = lax.rem(height + step, Z * NARROW)
        to_n, to_z = lax.div(to, Z), lax.rem(to, Z)
        return to, to_n, to_z, (column * Z + to_z) * CORES + core

    def remote(src, dst, send_sem, recv_sem, to_wide, to_narrow):
        return pltpu.make_async_remote_copy(
            src_ref=src,
            dst_ref=dst,
            send_sem=send_sem,
            recv_sem=recv_sem,
            device_id={"wide": to_wide, "narrow": to_narrow},
            device_id_type=MESH,
        )

    def send(*what):
        copy = remote(*what)
        copy.start()
        return copy

    barrier = pltpu.get_barrier_semaphore()

    def greet_ring(step, carry):
        _, to_n, _, to_wide = in_ring(step)
        pl.semaphore_signal(
            barrier, inc=1, device_id={"wide": to_wide, "narrow": to_n}, device_id_type=MESH
        )
        return carry

    def greet_plane(step, carry):
        _, _, _, to_wide = in_plane(step)
        pl.semaphore_signal(
            barrier, inc=1, device_id={"wide": to_wide, "narrow": n}, device_id_type=MESH
        )
        return carry

    lax.fori_loop(1, Z * NARROW, greet_ring, 0)
    lax.fori_loop(1, PLANE, greet_plane, 0)

    own = [
        pltpu.make_async_copy(draws_prev, d1.at[0], own_sem.at[0]),
        pltpu.make_async_copy(draws_panel, dv.at[0, 0], own_sem.at[1]),
        pltpu.make_async_copy(inverse, dv.at[1, 0], own_sem.at[2]),
        pltpu.make_async_copy(factor.at[pl.ds(128 * n, 128)], f_rows.at[0], own_sem.at[3]),
        pltpu.make_async_copy(corr.at[pl.ds(128 * n, 128)], c_rows.at[n], own_sem.at[4]),
    ]
    for copy in own:
        copy.start()
    for copy in own:
        copy.wait()
    pl.semaphore_wait(barrier, Z * NARROW - 1 + PLANE - 1)

    rows8 = pl.ds(8 * place, 8)
    rows8_core = pl.ds(8 * (4 * a + b), 8)
    rows16 = pl.ds(16 * place, 16)
    d_copies = []
    for k in (2, 1, 3):
        peer = rem4(n + k)
        d_copies.append(
            send(d1.at[0, rows8], d1.at[4 - k, rows8], d_send.at[k - 1, 0], d_recv.at[k - 1, 0], wide, peer)
        )
        d_copies.append(
            send(
                dv.at[core, 0, rows8_core],
                dv.at[core, 4 - k, rows8_core],
                d_send.at[k - 1, 1],
                d_recv.at[k - 1, 1],
                wide,
                peer,
            )
        )

    def to_plane(to):
        to_core, to_a, to_b = to // 16, (to // 4) % 4, to % 4
        to_x, to_y = (to_a, to_b) if to_core else (to_b, to_a)
        rows = pl.ds(16 * to, 16)
        return remote(
            factor.at[rows], piv.at[0, rows], p1_send.at[to], p1_recv, wide_of(to_x, to_y, 1, to_core), n
        )

    @pl.when(wide == OWNER)
    def _():
        for to in range(1, PLANE):
            to_plane(to).start()
        local = pltpu.make_async_copy(factor.at[pl.ds(0, 16)], piv.at[0, pl.ds(0, 16)], p1_send.at[0])
        local.start()
        local.wait()

    @pl.when((z == 1) & (wide != OWNER))
    def _():
        pltpu.make_async_copy(piv.at[0, rows16], piv.at[0, rows16], p1_recv).wait()

    def along_z(k, z_other):
        return remote(
            piv.at[0, rows16],
            piv.at[(4 - k) % 4, rows16],
            p2_send.at[k, z_other],
            p2_recv.at[(4 - k) % 4],
            wide_of(x, y, z_other, core),
            rem4(n + k),
        )

    others = [(k, z_other) for k in (2, 1, 3, 0) for z_other in range(Z) if (k, z_other) != (0, 1)]

    @pl.when(z == 1)
    def _():
        for k, z_other in others:
            along_z(k, z_other).start()

    def piece(kind, first, count):
        if kind == 0:
            return d1.at[pl.ds(1, 3), pl.ds(8 * first, 8 * count)]
        if kind == 1:
            return dv.at[core, pl.ds(1, 3), pl.ds(8 * (first - 16 * core), 8 * count)]
        return piv.at[:, pl.ds(16 * first, 16 * count)]

    def along(step, use_y):
        return wide_of(rem4(x + step * (1 - use_y)), rem4(y + step * use_y), z, core)

    def gather_first(kind):
        ref = piece(kind, place, 1)
        return [
            send(ref, ref, g1_send.at[step - 1, kind], g1_recv.at[step - 1, kind], along(step, core), n)
            for step in (1, 3, 2)
        ]

    partner = wide_of(x, y, z, 1 - core)

    def to_partner(kind, group, index):
        ref = piece(kind, 16 * core + 4 * group, 4)
        return send(ref, ref, x_send.at[index, kind], x_recv.at[index, kind], partner, n)

    def gather_second(kind):
        ref = piece(kind, 16 * core + 4 * a, 4)
        return [
            send(ref, ref, g2_send.at[step - 1, kind], g2_recv.at[step - 1, kind], along(step, 1 - core), n)
            for step in (1, 3, 2)
        ]

    for copy in d_copies:
        copy.wait_recv()
    first_d = [gather_first(0), gather_first(1)]
    for slot in range(1, NARROW):
        pltpu.make_async_copy(piv.at[slot, rows16], piv.at[slot, rows16], p2_recv.at[slot]).wait()

    @pl.when(z != 1)
    def _():
        pltpu.make_async_copy(piv.at[0, rows16], piv.at[0, rows16], p2_recv.at[0]).wait()

    f_copies, c_copies = {}, {}
    for k in (2, 1, 3):
        peer = rem4(n + k)
        rows = pl.ds(128 * peer, 128)
        c_copies[k] = send(corr.at[rows], c_rows.at[n], f_send.at[k - 1, 1], f_recv.at[k - 1, 1], wide, peer)
        f_copies[k] = send(
            factor.at[rows], f_rows.at[4 - k], f_send.at[k - 1, 0], f_recv.at[k - 1, 0], wide, peer
        )
    first_p = gather_first(2)

    second, core_copies = [], []
    for kind in (0, 1):
        for copy in first_d[kind]:
            copy.wait()
        second.append(gather_second(kind))
        core_copies.append(to_partner(kind, a, 0))
    for copy in first_p:
        copy.wait()
    second.append(gather_second(2))
    core_copies.append(to_partner(2, a, 0))
    for kind in range(3):
        for order, step in enumerate((1, 3, 2)):
            second[kind][order].wait_recv()
            core_copies.append(to_partner(kind, rem4(a + 4 - step), step))
    for copy in d_copies:
        copy.wait_send()
    for copies in second:
        for copy in copies:
            copy.wait_send()
    for copy in core_copies:
        copy.wait()

    @pl.when(wide == OWNER)
    def _():
        for to in range(1, PLANE):
            to_plane(to).wait_send()

    @pl.when(z == 1)
    def _():
        for k, z_other in others:
            along_z(k, z_other).wait_send()

    for k in range(NARROW):
        piv_split[0, k], piv_split[1, k] = split(piv[k])
        d1_split[0, k], d1_split[1, k] = split(d1[k])
        for which in range(2):
            dv_split[0, which, k], dv_split[1, which, k] = split(dv[which, k])

    product = jnp.zeros((128, 512), jnp.float32)
    sums = jnp.zeros((128, 512), jnp.float32)
    squares = jnp.zeros((128, 1), jnp.float32)
    for k in (0, 1, 3, 2):
        if k:
            f_copies[4 - k].wait_recv()
        part = f_rows[k]
        squares = squares + jnp.sum(part * part, axis=1, keepdims=True)
        part = split(part)
        product = product + dot3(part, (piv_split[0, k], piv_split[1, k]), 1, 1)
        sums = sums + dot3(part, (d1_split[0, k], d1_split[1, k]), 1, 0)
    for k in (1, 3, 2):
        c_copies[k].wait_recv()
    for m in range(NARROW):
        updated[:, 128 * m : 128 * m + 128] = c_rows[m] - product[:, 128 * m : 128 * m + 128]
    new = split(updated[...])
    for k in range(NARROW):
        value = dot3(new, (dv_split[0, 1, k], dv_split[1, 1, k]), 1, 1)
        panel[k] = value
        squares = squares + jnp.sum(value * value, axis=1, keepdims=True)
        sums = sums + dot3(split(value), (dv_split[0, 0, k], dv_split[1, 0, k]), 1, 0)
    scaled = sums * lax.rsqrt(squares + 1e-06)
    uniforms = 0.5 * (1.0 + lax.erf(scaled * HALF_ROOT))
    for m in range(NARROW):
        uni[m] = uniforms[:, 128 * m : 128 * m + 128].T.reshape(X * Y, Z, CORES, 1, 128)

    def up(step, carry):
        to, to_n, to_z, to_wide = in_ring(lax.rem(7 * step, Z * NARROW))
        remote(
            uni.at[to_n, :, to_z], mixed.at[:, :, z, n], u_send.at[to], u_recv.at[height], to_wide, to_n
        ).start()
        return carry

    lax.fori_loop(1, Z * NARROW, up, 0)
    q_copies = []
    for k in (2, 1, 3):
        q_copies.append(
            send(
                panel.at[k],
                panel_out.at[pl.ds(128 * n, 128)],
                q_send.at[k - 1],
                q_recv.at[k - 1],
                wide,
                rem4(n + k),
            )
        )
    local = pltpu.make_async_copy(uni.at[n, :, z], mixed.at[:, :, z, n], own_sem.at[0])
    local.start()
    panel_out[pl.ds(pl.multiple_of(128 * n, 128), 128), :] = panel[0]
    local.wait()

    def up_done(step, carry):
        to, to_n, to_z, to_wide = in_ring(step)
        copy = remote(
            uni.at[to_n, :, to_z], mixed.at[:, :, to_z, to_n], u_send.at[to], u_recv.at[to], to_wide, to_n
        )
        copy.wait()
        return carry

    lax.fori_loop(1, Z * NARROW, up_done, 0)

    def hand_out(step, carry):
        to, to_column, to_core, to_wide = in_plane(step)
        remote(
            mixed.at[to_column, to_core], full.at[column, :, core], a_send.at[to], a_recv.at[flat], to_wide, n
        ).start()
        return carry

    lax.fori_loop(1, PLANE, hand_out, 0)
    local = pltpu.make_async_copy(mixed.at[column, core], full.at[column, :, core], own_sem.at[1])
    local.start()
    local.wait()

    def handed(step, carry):
        to, to_column, to_core, to_wide = in_plane(step)
        remote(
            mixed.at[to_column, to_core],
            full.at[to_column, :, to_core],
            a_send.at[to],
            a_recv.at[to],
            to_wide,
            n,
        ).wait()
        return carry

    lax.fori_loop(1, PLANE, handed, 0)

    now = full[...].reshape(512, 128)
    row = lax.broadcasted_iota(jnp.int32, (512, 128), 0)
    lane = lax.broadcasted_iota(jnp.int32, (512, 128), 1)
    before = jnp.where(row == 0, 0.0, pltpu.roll(now, 1, 0))
    after = jnp.where(row == 511, 0.0, pltpu.roll(now, 511, 0))
    total = 6.0 / 16.0 * now
    for shift, weight in ((1, 4.0 / 16.0), (2, 1.0 / 16.0)):
        left = jnp.where(lane < shift, pltpu.roll(before, shift, 1), pltpu.roll(now, shift, 1))
        right = jnp.where(lane >= 128 - shift, pltpu.roll(after, 128 - shift, 1), pltpu.roll(now, 128 - shift, 1))
        total = total + weight * (left + right)
    smooth_out[...] = total
    for k in (1, 2, 3):
        f_copies[k].wait_send()
        c_copies[k].wait_send()
    for copy in q_copies:
        copy.wait()


def per_device(corr_panel, factor_prev, draws_prev, draws_panel, diag_inverse):
    anywhere = pl.BlockSpec(memory_space=pl.ANY)
    vmem = pl.BlockSpec(memory_space=pltpu.VMEM)
    dma = pltpu.SemaphoreType.DMA
    panel_factor, smoothed = pl.pallas_call(
        kernel,
        name="panel",
        out_shape=(
            jax.ShapeDtypeStruct((512, 128), jnp.float32),
            jax.ShapeDtypeStruct((512, 128), jnp.float32),
        ),
        in_specs=[anywhere] * 5,
        out_specs=(vmem, vmem),
        scratch_shapes=[
            pltpu.VMEM((4, 128, 256), jnp.float32),
            pltpu.VMEM((4, 128, 128), jnp.float32),
            pltpu.VMEM((4, 256, 512), jnp.float32),
            pltpu.VMEM((2, 4, 128, 512), jnp.float32),
            pltpu.VMEM((4, 512, 256), jnp.float32),
            pltpu.VMEM((2, 4, 256, 512), jnp.bfloat16),
            pltpu.VMEM((2, 2, 4, 128, 512), jnp.bfloat16),
            pltpu.VMEM((2, 4, 512, 256), jnp.bfloat16),
            pltpu.VMEM((128, 512), jnp.float32),
            pltpu.VMEM((4, 128, 128), jnp.float32),
            pltpu.VMEM((4, X * Y, Z, CORES, 1, 128), jnp.float32),
            pltpu.VMEM((X * Y, CORES, Z, NARROW, 1, 128), jnp.float32),
            pltpu.VMEM((X * Y, Z, CORES, NARROW, 1, 128), jnp.float32),
            dma((5,)),
            dma((3, 2)),
            dma((3, 2)),
            dma((PLANE,)),
            dma,
            dma((4, 4)),
            dma((4,)),
            dma((3, 2)),
            dma((3, 2)),
            dma((3, 3)),
            dma((3, 3)),
            dma((3, 3)),
            dma((3, 3)),
            dma((4, 3)),
            dma((4, 3)),
            dma((3,)),
            dma((3,)),
            dma((16,)),
            dma((16,)),
            dma((PLANE,)),
            dma((PLANE,)),
        ],
        compiler_params=pltpu.CompilerParams(
            collective_id=0, has_side_effects=True, vmem_limit_bytes=67043328
        ),
    )(corr_panel, factor_prev, draws_prev, draws_panel, diag_inverse)
    return panel_factor, smoothed.reshape(1, 512 * 128)


def solution(mesh):
    in_specs = (
        P("wide", "narrow"),
        P("wide", "narrow"),
        P("narrow", None),
        P("narrow", None),
        P("narrow", None),
    )
    out_specs = (P("wide", "narrow"), P(("narrow", "wide"), None))
    return jax.shard_map(
        per_device, mesh=mesh, in_specs=in_specs, out_specs=out_specs, check_vma=False
    )
```

```python
import functools
import math

import jax
import jax.numpy as jnp
from jax import lax
from jax.experimental import pallas as pl
from jax.experimental.pallas import tpu as pltpu
from jax.sharding import PartitionSpec as P

MESH = pl.DeviceIdType.MESH
HALF_ROOT = 1.0 / math.sqrt(2.0)
X, Y, Z, CORES = 4, 4, 4, 2
WIDE = X * Y * Z * CORES
NARROW = 4
OWNER = 2
PLANE = X * Y * CORES


def wide_of(x, y, z, core):
    return ((x * Y + y) * Z + z) * CORES + core


def rem4(value):
    return lax.rem(value, 4)


def dot(left, right, left_dim, right_dim):
    return lax.dot_general(
        left,
        right,
        (((left_dim,), (right_dim,)), ((), ())),
        preferred_element_type=jnp.float32,
    )


def split(value):
    head = value.astype(jnp.bfloat16)
    return head, (value - head.astype(jnp.float32)).astype(jnp.bfloat16)


def dot3(left, right, left_dim, right_dim):
    return dot(left[0], right[0], left_dim, right_dim) + (
        dot(left[0], right[1], left_dim, right_dim) + dot(left[1], right[0], left_dim, right_dim)
    )


def kernel(
    corr,
    factor,
    draws_prev,
    draws_panel,
    inverse,
    panel_out,
    smooth_out,
    f_rows,
    c_rows,
    d1,
    dv,
    piv,
    d1_split,
    dv_split,
    piv_split,
    updated,
    panel,
    uni,
    mixed,
    full,
    result,
    own_sem,
    d_send,
    d_recv,
    p1_send,
    p1_recv,
    p2_send,
    p2_recv,
    f_send,
    f_recv,
    g1_send,
    g1_recv,
    g2_send,
    g2_recv,
    x_send,
    x_recv,
    q_send,
    q_recv,
    u_send,
    u_recv,
    a_send,
    a_recv,
):
    wide = lax.axis_index("wide")
    n = lax.axis_index("narrow")
    core = lax.rem(wide, CORES)
    z = rem4(lax.div(wide, CORES))
    y = rem4(lax.div(wide, CORES * Z))
    x = lax.div(wide, CORES * Z * Y)
    a = core * x + (1 - core) * y
    b = core * y + (1 - core) * x
    place = 16 * core + 4 * a + b
    column = x * Y + y
    flat = column * CORES + core
    height = n * Z + z

    def in_plane(step):
        to = lax.rem(flat + step, PLANE)
        to_column, to_core = lax.div(to, CORES), lax.rem(to, CORES)
        return to, to_column, to_core, (to_column * Z + z) * CORES + to_core

    def in_ring(step):
        to = lax.rem(height + step, Z * NARROW)
        to_n, to_z = lax.div(to, Z), lax.rem(to, Z)
        return to, to_n, to_z, (column * Z + to_z) * CORES + core

    def remote(src, dst, send_sem, recv_sem, to_wide, to_narrow):
        return pltpu.make_async_remote_copy(
            src_ref=src,
            dst_ref=dst,
            send_sem=send_sem,
            recv_sem=recv_sem,
            device_id={"wide": to_wide, "narrow": to_narrow},
            device_id_type=MESH,
        )

    def send(*what):
        copy = remote(*what)
        copy.start()
        return copy

    own = [
        pltpu.make_async_copy(draws_prev, d1.at[0], own_sem.at[0]),
        pltpu.make_async_copy(draws_panel, dv.at[0, 0], own_sem.at[1]),
        pltpu.make_async_copy(inverse, dv.at[1, 0], own_sem.at[2]),
        pltpu.make_async_copy(factor.at[pl.ds(128 * n, 128)], f_rows.at[0], own_sem.at[3]),
        pltpu.make_async_copy(corr.at[pl.ds(128 * n, 128)], c_rows.at[n], own_sem.at[4]),
    ]
    for copy in own:
        copy.start()

    barrier = pltpu.get_barrier_semaphore()

    def greet(to_wide, to_n):
        pl.semaphore_signal(
            barrier, inc=1, device_id={"wide": to_wide, "narrow": to_n}, device_id_type=MESH
        )

    turned = [[rem4(at + step) for step in range(4)] for at in (x, y, z, n)]
    for step in range(1, Z * NARROW):
        greet(wide_of(x, y, turned[2][step % 4], core), turned[3][step // 4])
    for step in range(1, PLANE):
        greet(
            wide_of(turned[0][step // 8], turned[1][step // 2 % 4], z, core if step % 2 == 0 else 1 - core), n
        )
    pl.semaphore_wait(barrier, Z * NARROW - 1 + PLANE - 1)
    for copy in own:
        copy.wait()

    rows8 = pl.ds(8 * place, 8)
    rows8_core = pl.ds(8 * (4 * a + b), 8)
    rows16 = pl.ds(16 * place, 16)
    d_copies = []
    for k in (2, 1, 3):
        peer = rem4(n + k)
        d_copies.append(
            send(
                d1.at[0, rows8],
                d1.at[4 - k, rows8],
                d_send.at[k - 1, 0],
                d_recv.at[k - 1, 0],
                wide,
                peer,
            )
        )
        d_copies.append(
            send(
                dv.at[core, 0, rows8_core],
                dv.at[core, 4 - k, rows8_core],
                d_send.at[k - 1, 1],
                d_recv.at[k - 1, 1],
                wide,
                peer,
            )
        )

    def trade(k, kind):
        peer = rem4(n + k)
        rows = pl.ds(128 * peer, 128)
        src, dst = (factor.at[rows], f_rows.at[4 - k]) if kind == 0 else (corr.at[rows], c_rows.at[n])
        return remote(src, dst, f_send.at[k - 1, kind], f_recv.at[k - 1, kind], wide, peer)

    @pl.when(z != 1)
    def _():
        for k in (2, 1, 3):
            trade(k, 1).start()

    def to_plane(to):
        to_core, to_a, to_b = to // 16, (to // 4) % 4, to % 4
        to_x, to_y = (to_a, to_b) if to_core else (to_b, to_a)
        rows = pl.ds(16 * to, 16)
        return remote(
            factor.at[rows], piv.at[0, rows], p1_send.at[to], p1_recv, wide_of(to_x, to_y, 1, to_core), n
        )

    @pl.when(wide == OWNER)
    def _():
        for to in range(1, PLANE):
            to_plane(to).start()
        local = pltpu.make_async_copy(factor.at[pl.ds(0, 16)], piv.at[0, pl.ds(0, 16)], p1_send.at[0])
        local.start()
        local.wait()

    @pl.when((z == 1) & (wide != OWNER))
    def _():
        pltpu.make_async_copy(piv.at[0, rows16], piv.at[0, rows16], p1_recv).wait()

    def along_z(k, z_other):
        return remote(
            piv.at[0, rows16],
            piv.at[(4 - k) % 4, rows16],
            p2_send.at[k, z_other],
            p2_recv.at[(4 - k) % 4],
            wide_of(x, y, z_other, core),
            rem4(n + k),
        )

    others = [(k, z_other) for k in (2, 1, 3, 0) for z_other in range(Z) if (k, z_other) != (0, 1)]

    @pl.when(z == 1)
    def _():
        for k, z_other in others:
            along_z(k, z_other).start()
        for k in (2, 1, 3):
            trade(k, 1).start()

    def piece(kind, first, count):
        if kind == 0:
            return d1.at[pl.ds(1, 3), pl.ds(8 * first, 8 * count)]
        if kind == 1:
            return dv.at[core, pl.ds(1, 3), pl.ds(8 * (first - 16 * core), 8 * count)]
        return piv.at[:, pl.ds(16 * first, 16 * count)]

    def along(step, use_y):
        return wide_of(rem4(x + step * (1 - use_y)), rem4(y + step * use_y), z, core)

    def gather_first(kind):
        ref = piece(kind, place, 1)
        return [
            send(ref, ref, g1_send.at[step - 1, kind], g1_recv.at[step - 1, kind], along(step, core), n)
            for step in (1, 3, 2)
        ]

    partner = wide_of(x, y, z, 1 - core)

    def to_partner(kind, group, index):
        ref = piece(kind, 16 * core + 4 * group, 4)
        return send(ref, ref, x_send.at[index, kind], x_recv.at[index, kind], partner, n)

    def gather_second(kind):
        ref = piece(kind, 16 * core + 4 * a, 4)
        return [
            send(ref, ref, g2_send.at[step - 1, kind], g2_recv.at[step - 1, kind], along(step, 1 - core), n)
            for step in (1, 3, 2)
        ]

    for copy in d_copies:
        copy.wait_recv()
    first_d = [gather_first(0), gather_first(1)]
    for slot in range(1, NARROW):
        pltpu.make_async_copy(piv.at[slot, rows16], piv.at[slot, rows16], p2_recv.at[slot]).wait()

    @pl.when(z != 1)
    def _():
        pltpu.make_async_copy(piv.at[0, rows16], piv.at[0, rows16], p2_recv.at[0]).wait()

    f_copies = {k: trade(k, 0) for k in (2, 1, 3)}
    c_copies = {k: trade(k, 1) for k in (2, 1, 3)}
    for k in (2, 1, 3):
        f_copies[k].start()
    first_p = gather_first(2)

    second, core_copies = [], []
    for kind in (0, 1):
        for copy in first_d[kind]:
            copy.wait()
        second.append(gather_second(kind))
        core_copies.append(to_partner(kind, a, 0))
    for copy in first_p:
        copy.wait()
    second.append(gather_second(2))
    core_copies.append(to_partner(2, a, 0))
    for kind in range(3):
        for order, step in enumerate((1, 3, 2)):
            second[kind][order].wait_recv()
            core_copies.append(to_partner(kind, rem4(a + 4 - step), step))
    for copy in d_copies:
        copy.wait_send()
    for copies in second:
        for copy in copies:
            copy.wait_send()
    for copy in core_copies:
        copy.wait()

    @pl.when(wide == OWNER)
    def _():
        for to in range(1, PLANE):
            to_plane(to).wait_send()

    @pl.when(z == 1)
    def _():
        for k, z_other in others:
            along_z(k, z_other).wait_send()

    for k in range(NARROW):
        piv_split[0, k], piv_split[1, k] = split(piv[k])
        d1_split[0, k], d1_split[1, k] = split(d1[k])
        for which in range(2):
            dv_split[0, which, k], dv_split[1, which, k] = split(dv[which, k])

    product = jnp.zeros((128, 512), jnp.float32)
    sums = jnp.zeros((128, 512), jnp.float32)
    squares = jnp.zeros((128, 1), jnp.float32)
    for k in (0, 1, 3, 2):
        if k:
            f_copies[4 - k].wait_recv()
        part = f_rows[k]
        squares = squares + jnp.sum(part * part, axis=1, keepdims=True)
        part = split(part)
        product = product + dot3(part, (piv_split[0, k], piv_split[1, k]), 1, 1)
        sums = sums + dot3(part, (d1_split[0, k], d1_split[1, k]), 1, 0)
    for k in (1, 3, 2):
        c_copies[k].wait_recv()
    for m in range(NARROW):
        updated[:, 128 * m : 128 * m + 128] = c_rows[m] - product[:, 128 * m : 128 * m + 128]
    new = split(updated[...])
    inverse_split = tuple(dv_split[part, 1].reshape(512, 512) for part in range(2))
    draws_split = tuple(dv_split[part, 0].reshape(512, 512) for part in range(2))
    value = dot3(new, inverse_split, 1, 1)
    for k in range(NARROW):
        panel[k] = value[:, 128 * k : 128 * k + 128]
    squares = squares + jnp.sum(value * value, axis=1, keepdims=True)
    sums = sums + dot3(split(value), draws_split, 1, 0)
    scaled = sums * lax.rsqrt(squares + 1e-06)
    uniforms = 0.5 * (1.0 + lax.erf(scaled * HALF_ROOT))
    for m in range(NARROW):
        uni[m] = uniforms[:, 128 * m : 128 * m + 128].T.reshape(X * Y, Z, CORES, 1, 128)

    def up(step, carry):
        to, to_n, to_z, to_wide = in_ring(lax.rem(7 * step, Z * NARROW))
        remote(
            uni.at[to_n, :, to_z], mixed.at[:, :, z, n], u_send.at[to], u_recv.at[height], to_wide, to_n
        ).start()
        return carry

    lax.fori_loop(1, Z * NARROW, up, 0)
    q_copies = {
        k: remote(
            panel.at[k], panel_out.at[pl.ds(128 * n, 128)], q_send.at[k - 1], q_recv.at[k - 1], wide, rem4(n + k)
        )
        for k in (1, 2, 3)
    }
    q_copies[1].start()
    q_copies[3].start()
    local = pltpu.make_async_copy(uni.at[n, :, z], mixed.at[:, :, z, n], own_sem.at[0])
    local.start()
    kept = pltpu.make_async_copy(panel.at[0], panel_out.at[pl.ds(128 * n, 128)], own_sem.at[2])
    kept.start()
    local.wait()

    def up_done(step, carry):
        to, to_n, to_z, to_wide = in_ring(step)
        copy = remote(
            uni.at[to_n, :, to_z], mixed.at[:, :, to_z, to_n], u_send.at[to], u_recv.at[to], to_wide, to_n
        )
        copy.wait()
        return carry

    lax.fori_loop(1, Z * NARROW, up_done, 0)

    def hand_out(step, carry):
        to, to_column, to_core, to_wide = in_plane(step)
        remote(
            mixed.at[to_column, to_core], full.at[column, :, core], a_send.at[to], a_recv.at[flat], to_wide, n
        ).start()
        return carry

    lax.fori_loop(1, PLANE, hand_out, 0)
    q_copies[2].start()
    local = pltpu.make_async_copy(mixed.at[column, core], full.at[column, :, core], own_sem.at[1])
    local.start()
    local.wait()

    def handed(step, carry):
        to, to_column, to_core, to_wide = in_plane(step)
        remote(
            mixed.at[to_column, to_core],
            full.at[to_column, :, to_core],
            a_send.at[to],
            a_recv.at[to],
            to_wide,
            n,
        ).wait()
        return carry

    lax.fori_loop(1, PLANE, handed, 0)

    now = full[...].reshape(512, 128)
    row = lax.broadcasted_iota(jnp.int32, (512, 128), 0)
    lane = lax.broadcasted_iota(jnp.int32, (512, 128), 1)
    before = jnp.where(row == 0, 0.0, pltpu.roll(now, 1, 0))
    after = jnp.where(row == 511, 0.0, pltpu.roll(now, 511, 0))
    total = 6.0 / 16.0 * now
    for shift, weight in ((1, 4.0 / 16.0), (2, 1.0 / 16.0)):
        left = jnp.where(lane < shift, pltpu.roll(before, shift, 1), pltpu.roll(now, shift, 1))
        right = jnp.where(lane >= 128 - shift, pltpu.roll(after, 128 - shift, 1), pltpu.roll(now, 128 - shift, 1))
        total = total + weight * (left + right)
    result[...] = total
    done = pltpu.make_async_copy(result, smooth_out, own_sem.at[3])
    done.start()
    for k in (1, 2, 3):
        f_copies[k].wait_send()
        c_copies[k].wait_send()
    for k in (1, 2, 3):
        q_copies[k].wait()
    kept.wait()
    done.wait()


def per_device(corr_panel, factor_prev, draws_prev, draws_panel, diag_inverse):
    anywhere = pl.BlockSpec(memory_space=pl.ANY)
    dma = pltpu.SemaphoreType.DMA
    panel_factor, smoothed = pl.pallas_call(
        kernel,
        name="panel",
        out_shape=(
            jax.ShapeDtypeStruct((512, 128), jnp.float32),
            jax.ShapeDtypeStruct((512, 128), jnp.float32),
        ),
        in_specs=[anywhere] * 5,
        out_specs=(anywhere, anywhere),
        scratch_shapes=[
            pltpu.VMEM((4, 128, 256), jnp.float32),
            pltpu.VMEM((4, 128, 128), jnp.float32),
            pltpu.VMEM((4, 256, 512), jnp.float32),
            pltpu.VMEM((2, 4, 128, 512), jnp.float32),
            pltpu.VMEM((4, 512, 256), jnp.float32),
            pltpu.VMEM((2, 4, 256, 512), jnp.bfloat16),
            pltpu.VMEM((2, 2, 4, 128, 512), jnp.bfloat16),
            pltpu.VMEM((2, 4, 512, 256), jnp.bfloat16),
            pltpu.VMEM((128, 512), jnp.float32),
            pltpu.VMEM((4, 128, 128), jnp.float32),
            pltpu.VMEM((4, X * Y, Z, CORES, 1, 128), jnp.float32),
            pltpu.VMEM((X * Y, CORES, Z, NARROW, 1, 128), jnp.float32),
            pltpu.VMEM((X * Y, Z, CORES, NARROW, 1, 128), jnp.float32),
            pltpu.VMEM((512, 128), jnp.float32),
            dma((5,)),
            dma((3, 2)),
            dma((3, 2)),
            dma((PLANE,)),
            dma,
            dma((4, 4)),
            dma((4,)),
            dma((3, 2)),
            dma((3, 2)),
            dma((3, 3)),
            dma((3, 3)),
            dma((3, 3)),
            dma((3, 3)),
            dma((4, 3)),
            dma((4, 3)),
            dma((3,)),
            dma((3,)),
            dma((16,)),
            dma((16,)),
            dma((PLANE,)),
            dma((PLANE,)),
        ],
        compiler_params=pltpu.CompilerParams(
            collective_id=0, has_side_effects=True, vmem_limit_bytes=67043328
        ),
    )(corr_panel, factor_prev, draws_prev, draws_panel, diag_inverse)
    return panel_factor, smoothed.reshape(1, 512 * 128)


def solution(mesh):
    in_specs = (
        P("wide", "narrow"),
        P("wide", "narrow"),
        P("narrow", None),
        P("narrow", None),
        P("narrow", None),
    )
    out_specs = (P("wide", "narrow"), P(("narrow", "wide"), None))
    return jax.shard_map(
        per_device, mesh=mesh, in_specs=in_specs, out_specs=out_specs, check_vma=False
    )
```

```python
import functools
import math

import jax
import jax.numpy as jnp
from jax import lax
from jax.experimental import pallas as pl
from jax.experimental.pallas import tpu as pltpu
from jax.sharding import PartitionSpec as P

MESH = pl.DeviceIdType.MESH
HALF_ROOT = 1.0 / math.sqrt(2.0)
X, Y, Z, CORES = 4, 4, 4, 2
WIDE = X * Y * Z * CORES
NARROW = 4
OWNER = 2
PLANE = X * Y * CORES


def wide_of(x, y, z, core):
    return ((x * Y + y) * Z + z) * CORES + core


def rem4(value):
    return lax.rem(value, 4)


def dot(left, right, left_dim, right_dim):
    return lax.dot_general(
        left,
        right,
        (((left_dim,), (right_dim,)), ((), ())),
        preferred_element_type=jnp.float32,
    )


def split(value):
    head = value.astype(jnp.bfloat16)
    return head, (value - head.astype(jnp.float32)).astype(jnp.bfloat16)


def dot3(left, right, left_dim, right_dim):
    return dot(left[0], right[0], left_dim, right_dim) + (
        dot(left[0], right[1], left_dim, right_dim) + dot(left[1], right[0], left_dim, right_dim)
    )


def kernel(
    corr,
    factor,
    draws_prev,
    draws_panel,
    inverse,
    panel_out,
    smooth_out,
    f_rows,
    c_rows,
    d1,
    dv,
    piv,
    d1_split,
    dv_split,
    piv_split,
    updated,
    flat_uni,
    panel,
    uni,
    mixed,
    full,
    result,
    own_sem,
    d_send,
    d_recv,
    p1_send,
    p1_recv,
    p2_send,
    p2_recv,
    f_send,
    f_recv,
    g1_send,
    g1_recv,
    g2_send,
    g2_recv,
    x_send,
    x_recv,
    q_send,
    q_recv,
    u_send,
    u_recv,
    a_send,
    a_recv,
):
    wide = lax.axis_index("wide")
    n = lax.axis_index("narrow")
    core = lax.rem(wide, CORES)
    z = rem4(lax.div(wide, CORES))
    y = rem4(lax.div(wide, CORES * Z))
    x = lax.div(wide, CORES * Z * Y)
    a = core * x + (1 - core) * y
    b = core * y + (1 - core) * x
    place = 16 * core + 4 * a + b
    column = x * Y + y
    flat = column * CORES + core
    height = n * Z + z

    def in_plane(step):
        to = lax.rem(flat + step, PLANE)
        to_column, to_core = lax.div(to, CORES), lax.rem(to, CORES)
        return to, to_column, to_core, (to_column * Z + z) * CORES + to_core

    def in_ring(step):
        to = lax.rem(height + step, Z * NARROW)
        to_n, to_z = lax.div(to, Z), lax.rem(to, Z)
        return to, to_n, to_z, (column * Z + to_z) * CORES + core

    def remote(src, dst, send_sem, recv_sem, to_wide, to_narrow):
        return pltpu.make_async_remote_copy(
            src_ref=src,
            dst_ref=dst,
            send_sem=send_sem,
            recv_sem=recv_sem,
            device_id={"wide": to_wide, "narrow": to_narrow},
            device_id_type=MESH,
        )

    def send(*what):
        copy = remote(*what)
        copy.start()
        return copy

    own = [
        pltpu.make_async_copy(draws_prev, d1.at[0], own_sem.at[0]),
        pltpu.make_async_copy(draws_panel, dv.at[0, 0], own_sem.at[1]),
        pltpu.make_async_copy(inverse, dv.at[1, 0], own_sem.at[2]),
        pltpu.make_async_copy(factor.at[pl.ds(128 * n, 128)], f_rows.at[0], own_sem.at[3]),
        pltpu.make_async_copy(corr.at[pl.ds(128 * n, 128)], c_rows.at[n], own_sem.at[4]),
    ]
    for copy in own:
        copy.start()

    barrier = pltpu.get_barrier_semaphore()

    def greet(to_wide, to_n):
        pl.semaphore_signal(
            barrier, inc=1, device_id={"wide": to_wide, "narrow": to_n}, device_id_type=MESH
        )

    turned = [[rem4(at + step) for step in range(4)] for at in (x, y, z, n)]
    for step in range(1, Z * NARROW):
        greet(wide_of(x, y, turned[2][step % 4], core), turned[3][step // 4])
    for step in range(1, PLANE):
        greet(
            wide_of(turned[0][step // 8], turned[1][step // 2 % 4], z, core if step % 2 == 0 else 1 - core), n
        )
    pl.semaphore_wait(barrier, Z * NARROW - 1 + PLANE - 1)
    for copy in own:
        copy.wait()

    rows8 = pl.ds(8 * place, 8)
    rows8_core = pl.ds(8 * (4 * a + b), 8)
    rows16 = pl.ds(16 * place, 16)
    d_copies = []
    for k in (2, 1, 3):
        peer = rem4(n + k)
        d_copies.append(
            send(
                d1.at[0, rows8],
                d1.at[4 - k, rows8],
                d_send.at[k - 1, 0],
                d_recv.at[k - 1, 0],
                wide,
                peer,
            )
        )
        d_copies.append(
            send(
                dv.at[core, 0, rows8_core],
                dv.at[core, 4 - k, rows8_core],
                d_send.at[k - 1, 1],
                d_recv.at[k - 1, 1],
                wide,
                peer,
            )
        )

    def trade(k, kind):
        peer = rem4(n + k)
        if kind < 2:
            src = factor.at[pl.ds(128 * peer + 64 * kind, 64)]
            dst = f_rows.at[4 - k, pl.ds(64 * kind, 64)]
        else:
            src, dst = corr.at[pl.ds(128 * peer, 128)], c_rows.at[n]
        return remote(src, dst, f_send.at[k - 1, kind], f_recv.at[k - 1, kind], wide, peer)

    @pl.when(z != 1)
    def _():
        for k in (2, 1, 3):
            trade(k, 2).start()

    def to_plane(to):
        to_core, to_a, to_b = to // 16, (to // 4) % 4, to % 4
        to_x, to_y = (to_a, to_b) if to_core else (to_b, to_a)
        rows = pl.ds(16 * to, 16)
        return remote(
            factor.at[rows], piv.at[0, rows], p1_send, p1_recv, wide_of(to_x, to_y, 1, to_core), n
        )

    @pl.when(wide == OWNER)
    def _():
        for to in range(1, PLANE):
            to_plane(to).start()
        local = pltpu.make_async_copy(factor.at[pl.ds(0, 16)], piv.at[0, pl.ds(0, 16)], own_sem.at[0])
        local.start()
        local.wait()

    @pl.when((z == 1) & (wide != OWNER))
    def _():
        pltpu.make_async_copy(piv.at[0, rows16], piv.at[0, rows16], p1_recv).wait()

    def along_z(k, z_other):
        return remote(
            piv.at[0, rows16],
            piv.at[(4 - k) % 4, rows16],
            p2_send,
            p2_recv.at[(4 - k) % 4],
            wide_of(x, y, z_other, core),
            rem4(n + k),
        )

    others = [(k, z_other) for k in (2, 1, 3, 0) for z_other in range(Z) if (k, z_other) != (0, 1)]

    @pl.when(z == 1)
    def _():
        for k, z_other in others:
            along_z(k, z_other).start()
        for k in (2, 1, 3):
            trade(k, 2).start()

    def piece(kind, first, count):
        if kind == 0:
            return d1.at[pl.ds(1, 3), pl.ds(8 * first, 8 * count)]
        if kind == 1:
            return dv.at[core, pl.ds(1, 3), pl.ds(8 * (first - 16 * core), 8 * count)]
        return piv.at[:, pl.ds(16 * first, 16 * count)]

    def along(step, use_y):
        return wide_of(rem4(x + step * (1 - use_y)), rem4(y + step * use_y), z, core)

    def gather_first(kind):
        ref = piece(kind, place, 1)
        return [
            send(ref, ref, g1_send.at[step - 1, kind], g1_recv.at[step - 1, kind], along(step, core), n)
            for step in (1, 3, 2)
        ]

    partner = wide_of(x, y, z, 1 - core)

    def to_partner(kind, group, index):
        ref = piece(kind, 16 * core + 4 * group, 4)
        return send(ref, ref, x_send.at[index, kind], x_recv.at[index, kind], partner, n)

    def gather_second(kind):
        ref = piece(kind, 16 * core + 4 * a, 4)
        return [
            send(ref, ref, g2_send.at[step - 1, kind], g2_recv.at[step - 1, kind], along(step, 1 - core), n)
            for step in (1, 3, 2)
        ]

    for copy in d_copies:
        copy.wait_recv()
    first_d = [gather_first(0), gather_first(1)]
    for slot in range(1, NARROW):
        pltpu.make_async_copy(piv.at[slot, rows16], piv.at[slot, rows16], p2_recv.at[slot]).wait()

    @pl.when(z != 1)
    def _():
        pltpu.make_async_copy(piv.at[0, rows16], piv.at[0, rows16], p2_recv.at[0]).wait()

    f_copies = {(k, half): trade(k, half) for k in (2, 1, 3) for half in range(2)}
    c_copies = {k: trade(k, 2) for k in (2, 1, 3)}
    for half in range(2):
        for k in (2, 1, 3):
            f_copies[k, half].start()
    first_p = gather_first(2)

    second, core_copies = [], []
    for kind in (0, 1):
        for copy in first_d[kind]:
            copy.wait()
        second.append(gather_second(kind))
        core_copies.append(to_partner(kind, a, 0))
    for copy in first_p:
        copy.wait()
    second.append(gather_second(2))
    core_copies.append(to_partner(2, a, 0))
    for kind in range(3):
        for order, step in enumerate((1, 3, 2)):
            second[kind][order].wait_recv()
            core_copies.append(to_partner(kind, rem4(a + 4 - step), step))
    for copy in d_copies:
        copy.wait_send()
    for copies in second:
        for copy in copies:
            copy.wait_send()
    for copy in core_copies:
        copy.wait()

    @pl.when(wide == OWNER)
    def _():
        sent = piv.at[0, pl.ds(0, 16 * (PLANE - 1))]
        pltpu.make_async_copy(sent, sent, p1_send).wait()

    @pl.when(z == 1)
    def _():
        sent = piv.at[0, pl.ds(0, 16 * (Z * NARROW - 1))]
        pltpu.make_async_copy(sent, sent, p2_send).wait()

    for k in range(NARROW):
        piv_split[0, k], piv_split[1, k] = split(piv[k])
        d1_split[0, k], d1_split[1, k] = split(d1[k])
        for which in range(2):
            dv_split[0, which, k], dv_split[1, which, k] = split(dv[which, k])

    inverse_split = tuple(dv_split[part, 1].reshape(512, 512) for part in range(2))
    draws_split = tuple(dv_split[part, 0].reshape(512, 512) for part in range(2))
    q_copies = {
        (k, half): remote(
            panel.at[k, pl.ds(64 * half, 64)],
            panel_out.at[pl.ds(128 * n + 64 * half, 64)],
            q_send.at[k - 1, half],
            q_recv.at[k - 1, half],
            wide,
            rem4(n + k),
        )
        for k in (1, 2, 3)
        for half in range(2)
    }
    for half in range(2):
        rows = pl.ds(64 * half, 64)
        product = jnp.zeros((64, 512), jnp.float32)
        sums = jnp.zeros((64, 512), jnp.float32)
        squares = jnp.zeros((64, 1), jnp.float32)
        for k in (0, 1, 3, 2):
            if k:
                f_copies[4 - k, half].wait_recv()
            if half and k == 2:
                q_copies[2, 0].start()
            part = f_rows[k, rows]
            squares = squares + jnp.sum(part * part, axis=1, keepdims=True)
            part = split(part)
            product = product + dot3(part, (piv_split[0, k], piv_split[1, k]), 1, 1)
            sums = sums + dot3(part, (d1_split[0, k], d1_split[1, k]), 1, 0)
        if half == 0:
            for k in (1, 3, 2):
                c_copies[k].wait_recv()
        for m in range(NARROW):
            updated[:, 128 * m : 128 * m + 128] = c_rows[m, rows] - product[:, 128 * m : 128 * m + 128]
        value = dot3(split(updated[...]), inverse_split, 1, 1)
        for k in range(NARROW):
            panel[k, rows] = value[:, 128 * k : 128 * k + 128]
        squares = squares + jnp.sum(value * value, axis=1, keepdims=True)
        sums = sums + dot3(split(value), draws_split, 1, 0)
        scaled = sums * lax.rsqrt(squares + 1e-06)
        flat_uni[rows, :] = 0.5 * (1.0 + lax.erf(scaled * HALF_ROOT))
    for m in range(NARROW):
        uni[m] = flat_uni[:, 128 * m : 128 * m + 128].T.reshape(X * Y, Z, CORES, 1, 128)

    def up(step, carry):
        to, to_n, to_z, to_wide = in_ring(lax.rem(7 * step, Z * NARROW))
        remote(
            uni.at[to_n, :, to_z], mixed.at[:, :, z, n], u_send, u_recv, to_wide, to_n
        ).start()
        return carry

    lax.fori_loop(1, Z * NARROW, up, 0)
    q_copies[2, 1].start()
    local = pltpu.make_async_copy(uni.at[n, :, z], mixed.at[:, :, z, n], own_sem.at[0])
    local.start()
    kept = pltpu.make_async_copy(panel.at[0], panel_out.at[pl.ds(128 * n, 128)], own_sem.at[2])
    kept.start()
    local.wait()

    moved = mixed.at[pl.ds(0, Z * NARROW - 1)]
    pltpu.make_async_copy(moved, moved, u_recv).wait()
    pltpu.make_async_copy(moved, moved, u_send).wait()

    def hand_out(step, carry):
        to, to_column, to_core, to_wide = in_plane(step)
        remote(
            mixed.at[to_column, to_core], full.at[column, :, core], a_send, a_recv, to_wide, n
        ).start()
        return carry

    lax.fori_loop(1, PLANE, hand_out, 0)
    for half in range(2):
        for k in (1, 3):
            q_copies[k, half].start()
    local = pltpu.make_async_copy(mixed.at[column, core], full.at[column, :, core], own_sem.at[1])
    local.start()
    local.wait()

    moved = piv.at[0, pl.ds(0, 8 * (PLANE - 1))]
    pltpu.make_async_copy(moved, moved, a_recv).wait()
    pltpu.make_async_copy(moved, moved, a_send).wait()

    now = full[...].reshape(512, 128)
    row = lax.broadcasted_iota(jnp.int32, (512, 128), 0)
    lane = lax.broadcasted_iota(jnp.int32, (512, 128), 1)
    before = jnp.where(row == 0, 0.0, pltpu.roll(now, 1, 0))
    after = jnp.where(row == 511, 0.0, pltpu.roll(now, 511, 0))
    total = 6.0 / 16.0 * now
    for shift, weight in ((1, 4.0 / 16.0), (2, 1.0 / 16.0)):
        left = jnp.where(lane < shift, pltpu.roll(before, shift, 1), pltpu.roll(now, shift, 1))
        right = jnp.where(lane >= 128 - shift, pltpu.roll(after, 128 - shift, 1), pltpu.roll(now, 128 - shift, 1))
        total = total + weight * (left + right)
    smooth_out[...] = total
    for copy in (*f_copies.values(), *c_copies.values()):
        copy.wait_send()
    for copy in q_copies.values():
        copy.wait()
    kept.wait()


def per_device(corr_panel, factor_prev, draws_prev, draws_panel, diag_inverse):
    anywhere = pl.BlockSpec(memory_space=pl.ANY)
    dma = pltpu.SemaphoreType.DMA
    panel_factor, smoothed = pl.pallas_call(
        kernel,
        name="panel",
        out_shape=(
            jax.ShapeDtypeStruct((512, 128), jnp.float32),
            jax.ShapeDtypeStruct((512, 128), jnp.float32),
        ),
        in_specs=[anywhere] * 5,
        out_specs=(pl.BlockSpec(memory_space=pltpu.VMEM), pl.BlockSpec(memory_space=pltpu.VMEM)),
        scratch_shapes=[
            pltpu.VMEM((4, 128, 256), jnp.float32),
            pltpu.VMEM((4, 128, 128), jnp.float32),
            pltpu.VMEM((4, 256, 512), jnp.float32),
            pltpu.VMEM((2, 4, 128, 512), jnp.float32),
            pltpu.VMEM((4, 512, 256), jnp.float32),
            pltpu.VMEM((2, 4, 256, 512), jnp.bfloat16),
            pltpu.VMEM((2, 2, 4, 128, 512), jnp.bfloat16),
            pltpu.VMEM((2, 4, 512, 256), jnp.bfloat16),
            pltpu.VMEM((64, 512), jnp.float32),
            pltpu.VMEM((128, 512), jnp.float32),
            pltpu.VMEM((4, 128, 128), jnp.float32),
            pltpu.VMEM((4, X * Y, Z, CORES, 1, 128), jnp.float32),
            pltpu.VMEM((X * Y, CORES, Z, NARROW, 1, 128), jnp.float32),
            pltpu.VMEM((X * Y, Z, CORES, NARROW, 1, 128), jnp.float32),
            pltpu.VMEM((512, 128), jnp.float32),
            dma((5,)),
            dma((3, 2)),
            dma((3, 2)),
            dma,
            dma,
            dma,
            dma((4,)),
            dma((3, 3)),
            dma((3, 3)),
            dma((3, 3)),
            dma((3, 3)),
            dma((3, 3)),
            dma((3, 3)),
            dma((4, 3)),
            dma((4, 3)),
            dma((3, 2)),
            dma((3, 2)),
            dma,
            dma,
            dma,
            dma,
        ],
        compiler_params=pltpu.CompilerParams(
            collective_id=0, has_side_effects=True, vmem_limit_bytes=40 * 2**20
        ),
    )(*(pltpu.with_memory_space_constraint(v, pltpu.HBM) for v in (corr_panel, factor_prev, draws_prev, draws_panel, diag_inverse)))
    return panel_factor, smoothed.reshape(1, 512 * 128)


def solution(mesh):
    in_specs = (
        P("wide", "narrow"),
        P("wide", "narrow"),
        P("narrow", None),
        P("narrow", None),
        P("narrow", None),
    )
    out_specs = (P("wide", "narrow"), P(("narrow", "wide"), None))
    return jax.shard_map(
        per_device, mesh=mesh, in_specs=in_specs, out_specs=out_specs, check_vma=False
    )
```

```python
import functools
import math

import jax
import jax.numpy as jnp
from jax import lax
from jax.experimental import pallas as pl
from jax.experimental.pallas import tpu as pltpu
from jax.sharding import PartitionSpec as P

MESH = pl.DeviceIdType.MESH
HALF_ROOT = 1.0 / math.sqrt(2.0)
X, Y, Z, CORES = 4, 4, 4, 2
WIDE = X * Y * Z * CORES
NARROW = 4
OWNER = 2
PLANE = X * Y * CORES


def wide_of(x, y, z, core):
    return ((x * Y + y) * Z + z) * CORES + core


def rem4(value):
    return lax.rem(value, 4)


def dot(left, right, left_dim, right_dim):
    return lax.dot_general(
        left,
        right,
        (((left_dim,), (right_dim,)), ((), ())),
        preferred_element_type=jnp.float32,
    )


def split(value):
    head = value.astype(jnp.bfloat16)
    return head, (value - head.astype(jnp.float32)).astype(jnp.bfloat16)


def dot3(left, right, left_dim, right_dim):
    return dot(left[0], right[0], left_dim, right_dim) + (
        dot(left[0], right[1], left_dim, right_dim) + dot(left[1], right[0], left_dim, right_dim)
    )


def kernel(
    corr,
    factor,
    draws_prev,
    draws_panel,
    inverse,
    panel_out,
    smooth_out,
    f_rows,
    c_rows,
    d1,
    dv,
    piv,
    d1_split,
    dv_split,
    piv_split,
    updated,
    flat_uni,
    panel,
    uni,
    mixed,
    full,
    result,
    own_sem,
    d_send,
    d_recv,
    z_send,
    z_recv,
    p1_send,
    p1_recv,
    p2_send,
    p2_recv,
    f_send,
    f_recv,
    g1_send,
    g1_recv,
    g2_send,
    g2_recv,
    g3_send,
    g3_recv,
    x_send,
    x_recv,
    q_send,
    q_recv,
    u_send,
    u_recv,
    a_send,
    a_recv,
):
    wide = lax.axis_index("wide")
    n = lax.axis_index("narrow")
    core = lax.rem(wide, CORES)
    z = rem4(lax.div(wide, CORES))
    y = rem4(lax.div(wide, CORES * Z))
    x = lax.div(wide, CORES * Z * Y)
    a = core * x + (1 - core) * y
    b = core * y + (1 - core) * x
    place = 16 * core + 4 * a + b
    column = x * Y + y
    flat = column * CORES + core
    height = n * Z + z

    def in_plane(step):
        to = lax.rem(flat + step, PLANE)
        to_column, to_core = lax.div(to, CORES), lax.rem(to, CORES)
        return to, to_column, to_core, (to_column * Z + z) * CORES + to_core

    def in_ring(step):
        to = lax.rem(height + step, Z * NARROW)
        to_n, to_z = lax.div(to, Z), lax.rem(to, Z)
        return to, to_n, to_z, (column * Z + to_z) * CORES + core

    def remote(src, dst, send_sem, recv_sem, to_wide, to_narrow):
        return pltpu.make_async_remote_copy(
            src_ref=src,
            dst_ref=dst,
            send_sem=send_sem,
            recv_sem=recv_sem,
            device_id={"wide": to_wide, "narrow": to_narrow},
            device_id_type=MESH,
        )

    def send(*what):
        copy = remote(*what)
        copy.start()
        return copy

    own = [
        pltpu.make_async_copy(draws_prev, d1.at[0], own_sem.at[0]),
        pltpu.make_async_copy(draws_panel, dv.at[0, 0], own_sem.at[1]),
        pltpu.make_async_copy(inverse, dv.at[1, 0], own_sem.at[2]),
        pltpu.make_async_copy(factor.at[pl.ds(128 * n, 128)], f_rows.at[0], own_sem.at[3]),
        pltpu.make_async_copy(corr.at[pl.ds(128 * n, 128)], c_rows.at[n], own_sem.at[4]),
    ]
    for copy in own:
        copy.start()

    barrier = pltpu.get_barrier_semaphore()

    def greet(to_wide, to_n):
        pl.semaphore_signal(
            barrier, inc=1, device_id={"wide": to_wide, "narrow": to_n}, device_id_type=MESH
        )

    turned = [[rem4(at + step) for step in range(4)] for at in (x, y, z, n)]
    for step in range(1, Z * NARROW):
        greet(wide_of(x, y, turned[2][step % 4], core), turned[3][step // 4])
    for step in range(1, PLANE):
        greet(
            wide_of(turned[0][step // 8], turned[1][step // 2 % 4], z, core if step % 2 == 0 else 1 - core), n
        )
    pl.semaphore_wait(barrier, Z * NARROW - 1 + PLANE - 1)
    for copy in own:
        copy.wait()

    rows8 = pl.ds(8 * place, 8)
    rows8_core = pl.ds(8 * (4 * a + b), 8)
    rows16 = pl.ds(16 * place, 16)
    quarter = pl.ds(pl.multiple_of(128 * z, 128), 128)
    d_copies = []
    for k in (2, 1, 3):
        for kind, ref in enumerate((d1.at[:, rows8, quarter], dv.at[core, :, rows8_core, quarter])):
            d_copies.append(
                send(
                    ref.at[0], ref.at[4 - k], d_send.at[k - 1, kind], d_recv.at[k - 1, kind], wide, rem4(n + k)
                )
            )

    def trade(k, kind):
        peer = rem4(n + k)
        if kind < 2:
            src = factor.at[pl.ds(128 * peer + 64 * kind, 64)]
            dst = f_rows.at[4 - k, pl.ds(64 * kind, 64)]
        else:
            src, dst = corr.at[pl.ds(128 * peer, 128)], c_rows.at[n]
        return remote(src, dst, f_send.at[k - 1, kind], f_recv.at[k - 1, kind], wide, peer)

    @pl.when(z != 1)
    def _():
        trade(2, 2).start()

    def to_plane(to):
        to_core, to_a, to_b = to // 16, (to // 4) % 4, to % 4
        to_x, to_y = (to_a, to_b) if to_core else (to_b, to_a)
        rows = pl.ds(16 * to, 16)
        return remote(
            factor.at[rows], piv.at[0, rows], p1_send, p1_recv, wide_of(to_x, to_y, 1, to_core), n
        )

    @pl.when(wide == OWNER)
    def _():
        for to in range(1, PLANE):
            to_plane(to).start()
        local = pltpu.make_async_copy(factor.at[pl.ds(0, 16)], piv.at[0, pl.ds(0, 16)], own_sem.at[0])
        local.start()
        local.wait()

    @pl.when((z == 1) & (wide != OWNER))
    def _():
        pltpu.make_async_copy(piv.at[0, rows16], piv.at[0, rows16], p1_recv).wait()

    def along_z(k, z_other):
        return remote(
            piv.at[0, rows16],
            piv.at[(4 - k) % 4, rows16],
            p2_send,
            p2_recv.at[(4 - k) % 4],
            wide_of(x, y, z_other, core),
            rem4(n + k),
        )

    others = [(k, z_other) for k in (2, 1, 3, 0) for z_other in range(Z) if (k, z_other) != (0, 1)]

    @pl.when(z == 1)
    def _():
        for k, z_other in others:
            along_z(k, z_other).start()
        trade(2, 2).start()

    def piece(kind, first, count):
        if kind == 0:
            return d1.at[pl.ds(1, 3), pl.ds(8 * first, 8 * count)]
        if kind == 1:
            return dv.at[core, pl.ds(1, 3), pl.ds(8 * (first - 16 * core), 8 * count)]
        return piv.at[:, pl.ds(16 * first, 16 * count)]

    def along(step, use_y):
        return wide_of(rem4(x + step * (1 - use_y)), rem4(y + step * use_y), z, core)

    def gather_first(kind):
        ref = piece(kind, place, 1)
        return [
            send(ref, ref, g1_send.at[step - 1, kind], g1_recv.at[step - 1, kind], along(step, core), n)
            for step in (1, 3, 2)
        ]

    partner = wide_of(x, y, z, 1 - core)

    def to_partner(kind, group, index):
        ref = piece(kind, 16 * core + 4 * group, 4)
        return send(ref, ref, x_send.at[index, kind], x_recv.at[index, kind], partner, n)

    def gather_second(kind):
        ref = piece(kind, 16 * core + 4 * a, 4)
        return {
            step: send(ref, ref, g2_send.at[step // 2, kind], g2_recv.at[step // 2, kind], along(step, 1 - core), n)
            for step in (1, 3)
        }

    def pass_on(kind, step):
        group, half = rem4(a + 4 - step), step // 2
        ref = piece(kind, 16 * core + 4 * group + 2 * half, 2)
        return send(ref, ref, g3_send.at[half, kind], g3_recv.at[half, kind], along(step, 1 - core), n)

    for copy in d_copies:
        copy.wait_recv()
    z_copies = []
    for step in (1, 2, 3):
        to_wide = wide_of(x, y, rem4(z + step), core)
        for kind, ref in enumerate((d1.at[pl.ds(1, 3), rows8, quarter], dv.at[core, pl.ds(1, 3), rows8_core, quarter])):
            z_copies.append(send(ref, ref, z_send.at[step - 1, kind], z_recv.at[step - 1, kind], to_wide, n))
    trade(1, 2).start()
    trade(3, 2).start()
    for copy in z_copies:
        copy.wait()
    first_d = [gather_first(0), gather_first(1)]
    for slot in range(1, NARROW):
        pltpu.make_async_copy(piv.at[slot, rows16], piv.at[slot, rows16], p2_recv.at[slot]).wait()

    @pl.when(z != 1)
    def _():
        pltpu.make_async_copy(piv.at[0, rows16], piv.at[0, rows16], p2_recv.at[0]).wait()

    f_copies = {(k, half): trade(k, half) for k in (2, 1, 3) for half in range(2)}
    c_copies = {k: trade(k, 2) for k in (2, 1, 3)}
    for half in range(2):
        for k in (2, 1, 3):
            f_copies[k, half].start()
    first_p = gather_first(2)

    second, core_copies = [], []
    for kind in (0, 1):
        for copy in first_d[kind]:
            copy.wait()
        second.append(gather_second(kind))
        core_copies.append(to_partner(kind, a, 0))
    for copy in first_p:
        copy.wait()
    second.append(gather_second(2))
    core_copies.append(to_partner(2, a, 0))
    third = []
    for kind in range(3):
        for step in (1, 3):
            second[kind][step].wait_recv()
            third.append(pass_on(kind, step))
            core_copies.append(to_partner(kind, rem4(a + 4 - step), step))
    for kind in range(3):
        third[2 * kind].wait_recv()
        third[2 * kind + 1].wait_recv()
        core_copies.append(to_partner(kind, rem4(a + 2), 2))
    for copy in d_copies:
        copy.wait_send()
    for copies in second:
        copies[1].wait_send()
        copies[3].wait_send()
    for copy in third:
        copy.wait_send()
    for copy in core_copies:
        copy.wait()

    @pl.when(wide == OWNER)
    def _():
        sent = piv.at[0, pl.ds(0, 16 * (PLANE - 1))]
        pltpu.make_async_copy(sent, sent, p1_send).wait()

    @pl.when(z == 1)
    def _():
        sent = piv.at[0, pl.ds(0, 16 * (Z * NARROW - 1))]
        pltpu.make_async_copy(sent, sent, p2_send).wait()

    for k in range(NARROW):
        piv_split[0, k], piv_split[1, k] = split(piv[k])
        d1_split[0, k], d1_split[1, k] = split(d1[k])
        for which in range(2):
            dv_split[0, which, k], dv_split[1, which, k] = split(dv[which, k])

    inverse_split = tuple(dv_split[part, 1].reshape(512, 512) for part in range(2))
    draws_split = tuple(dv_split[part, 0].reshape(512, 512) for part in range(2))
    q_copies = {
        (k, half): remote(
            panel.at[k, pl.ds(64 * half, 64)],
            panel_out.at[pl.ds(128 * n + 64 * half, 64)],
            q_send.at[k - 1, half],
            q_recv.at[k - 1, half],
            wide,
            rem4(n + k),
        )
        for k in (1, 2, 3)
        for half in range(2)
    }
    for half in range(2):
        rows = pl.ds(64 * half, 64)
        product = jnp.zeros((64, 512), jnp.float32)
        sums = jnp.zeros((64, 512), jnp.float32)
        squares = jnp.zeros((64, 1), jnp.float32)
        for k in (0, 1, 3, 2):
            if k:
                f_copies[4 - k, half].wait_recv()
            if half and k == 2:
                q_copies[2, 0].start()
            part = f_rows[k, rows]
            squares = squares + jnp.sum(part * part, axis=1, keepdims=True)
            part = split(part)
            product = product + dot3(part, (piv_split[0, k], piv_split[1, k]), 1, 1)
            sums = sums + dot3(part, (d1_split[0, k], d1_split[1, k]), 1, 0)
        if half == 0:
            for k in (1, 3, 2):
                c_copies[k].wait_recv()
        for m in range(NARROW):
            updated[:, 128 * m : 128 * m + 128] = c_rows[m, rows] - product[:, 128 * m : 128 * m + 128]
        value = dot3(split(updated[...]), inverse_split, 1, 1)
        for k in range(NARROW):
            panel[k, rows] = value[:, 128 * k : 128 * k + 128]
        squares = squares + jnp.sum(value * value, axis=1, keepdims=True)
        sums = sums + dot3(split(value), draws_split, 1, 0)
        scaled = sums * lax.rsqrt(squares + 1e-06)
        flat_uni[rows, :] = 0.5 * (1.0 + lax.erf(scaled * HALF_ROOT))
    for m in range(NARROW):
        uni[m] = flat_uni[:, 128 * m : 128 * m + 128].T.reshape(X * Y, Z, CORES, 1, 128)

    def up(step, carry):
        to, to_n, to_z, to_wide = in_ring(lax.rem(7 * step, Z * NARROW))
        remote(
            uni.at[to_n, :, to_z], mixed.at[:, :, z, n], u_send, u_recv, to_wide, to_n
        ).start()
        return carry

    lax.fori_loop(1, Z * NARROW, up, 0)
    q_copies[2, 1].start()
    local = pltpu.make_async_copy(uni.at[n, :, z], mixed.at[:, :, z, n], own_sem.at[0])
    local.start()
    kept = pltpu.make_async_copy(panel.at[0], panel_out.at[pl.ds(128 * n, 128)], own_sem.at[2])
    kept.start()
    local.wait()

    moved = mixed.at[pl.ds(0, Z * NARROW - 1)]
    pltpu.make_async_copy(moved, moved, u_recv).wait()
    pltpu.make_async_copy(moved, moved, u_send).wait()

    def hand_out(step, carry):
        to, to_column, to_core, to_wide = in_plane(step)
        remote(
            mixed.at[to_column, to_core], full.at[column, :, core], a_send, a_recv, to_wide, n
        ).start()
        return carry

    lax.fori_loop(1, PLANE, hand_out, 0)
    for half in range(2):
        for k in (1, 3):
            q_copies[k, half].start()
    local = pltpu.make_async_copy(mixed.at[column, core], full.at[column, :, core], own_sem.at[1])
    local.start()
    local.wait()

    moved = piv.at[0, pl.ds(0, 8 * (PLANE - 1))]
    pltpu.make_async_copy(moved, moved, a_recv).wait()
    pltpu.make_async_copy(moved, moved, a_send).wait()

    now = full[...].reshape(512, 128)
    row = lax.broadcasted_iota(jnp.int32, (512, 128), 0)
    lane = lax.broadcasted_iota(jnp.int32, (512, 128), 1)
    before = jnp.where(row == 0, 0.0, pltpu.roll(now, 1, 0))
    after = jnp.where(row == 511, 0.0, pltpu.roll(now, 511, 0))
    total = 6.0 / 16.0 * now
    for shift, weight in ((1, 4.0 / 16.0), (2, 1.0 / 16.0)):
        left = jnp.where(lane < shift, pltpu.roll(before, shift, 1), pltpu.roll(now, shift, 1))
        right = jnp.where(lane >= 128 - shift, pltpu.roll(after, 128 - shift, 1), pltpu.roll(now, 128 - shift, 1))
        total = total + weight * (left + right)
    smooth_out[...] = total
    for copy in (*f_copies.values(), *c_copies.values()):
        copy.wait_send()
    for copy in q_copies.values():
        copy.wait()
    kept.wait()


def per_device(corr_panel, factor_prev, draws_prev, draws_panel, diag_inverse):
    anywhere = pl.BlockSpec(memory_space=pl.ANY)
    dma = pltpu.SemaphoreType.DMA
    panel_factor, smoothed = pl.pallas_call(
        kernel,
        name="panel",
        out_shape=(
            jax.ShapeDtypeStruct((512, 128), jnp.float32),
            jax.ShapeDtypeStruct((512, 128), jnp.float32),
        ),
        in_specs=[anywhere] * 5,
        out_specs=(pl.BlockSpec(memory_space=pltpu.VMEM), pl.BlockSpec(memory_space=pltpu.VMEM)),
        scratch_shapes=[
            pltpu.VMEM((4, 128, 256), jnp.float32),
            pltpu.VMEM((4, 128, 128), jnp.float32),
            pltpu.VMEM((4, 256, 512), jnp.float32),
            pltpu.VMEM((2, 4, 128, 512), jnp.float32),
            pltpu.VMEM((4, 512, 256), jnp.float32),
            pltpu.VMEM((2, 4, 256, 512), jnp.bfloat16),
            pltpu.VMEM((2, 2, 4, 128, 512), jnp.bfloat16),
            pltpu.VMEM((2, 4, 512, 256), jnp.bfloat16),
            pltpu.VMEM((64, 512), jnp.float32),
            pltpu.VMEM((128, 512), jnp.float32),
            pltpu.VMEM((4, 128, 128), jnp.float32),
            pltpu.VMEM((4, X * Y, Z, CORES, 1, 128), jnp.float32),
            pltpu.VMEM((X * Y, CORES, Z, NARROW, 1, 128), jnp.float32),
            pltpu.VMEM((X * Y, Z, CORES, NARROW, 1, 128), jnp.float32),
            pltpu.VMEM((512, 128), jnp.float32),
            dma((5,)),
            dma((3, 2)),
            dma((3, 2)),
            dma((3, 2)),
            dma((3, 2)),
            dma,
            dma,
            dma,
            dma((4,)),
            dma((3, 3)),
            dma((3, 3)),
            dma((3, 3)),
            dma((3, 3)),
            dma((2, 3)),
            dma((2, 3)),
            dma((2, 3)),
            dma((2, 3)),
            dma((4, 3)),
            dma((4, 3)),
            dma((3, 2)),
            dma((3, 2)),
            dma,
            dma,
            dma,
            dma,
        ],
        compiler_params=pltpu.CompilerParams(
            collective_id=0, has_side_effects=True, vmem_limit_bytes=40 * 2**20
        ),
    )(*(pltpu.with_memory_space_constraint(v, pltpu.HBM) for v in (corr_panel, factor_prev, draws_prev, draws_panel, diag_inverse)))
    return panel_factor, smoothed.reshape(1, 512 * 128)


def solution(mesh):
    in_specs = (
        P("wide", "narrow"),
        P("wide", "narrow"),
        P("narrow", None),
        P("narrow", None),
        P("narrow", None),
    )
    out_specs = (P("wide", "narrow"), P(("narrow", "wide"), None))
    return jax.shard_map(
        per_device, mesh=mesh, in_specs=in_specs, out_specs=out_specs, check_vma=False
    )
```

```python
import functools
import math

import jax
import jax.numpy as jnp
from jax import lax
from jax.experimental import pallas as pl
from jax.experimental.pallas import tpu as pltpu
from jax.sharding import PartitionSpec as P

MESH = pl.DeviceIdType.MESH
HALF_ROOT = 1.0 / math.sqrt(2.0)
X, Y, Z, CORES = 4, 4, 4, 2
WIDE = X * Y * Z * CORES
NARROW = 4
OWNER = 2
PLANE = X * Y * CORES


def wide_of(x, y, z, core):
    return ((x * Y + y) * Z + z) * CORES + core


def rem4(value):
    return lax.rem(value, 4)


def dot(left, right, left_dim, right_dim):
    return lax.dot_general(
        left,
        right,
        (((left_dim,), (right_dim,)), ((), ())),
        preferred_element_type=jnp.float32,
    )


def split(value):
    head = value.astype(jnp.bfloat16)
    return head, (value - head.astype(jnp.float32)).astype(jnp.bfloat16)


def dot3(left, right, left_dim, right_dim):
    return dot(left[0], right[0], left_dim, right_dim) + (
        dot(left[0], right[1], left_dim, right_dim) + dot(left[1], right[0], left_dim, right_dim)
    )


def kernel(
    corr,
    factor,
    draws_prev,
    draws_panel,
    inverse,
    panel_out,
    smooth_out,
    f_rows,
    c_rows,
    d1,
    dv,
    piv,
    d1_split,
    dv_split,
    piv_split,
    updated,
    flat_uni,
    panel,
    uni,
    mixed,
    full,
    result,
    own_sem,
    d_send,
    d_recv,
    z_send,
    z_recv,
    p1_send,
    p1_recv,
    p2_send,
    p2_recv,
    f_send,
    f_recv,
    g1_send,
    g1_recv,
    g2_send,
    g2_recv,
    g3_send,
    g3_recv,
    x_send,
    x_recv,
    q_send,
    q_recv,
    u_send,
    u_recv,
    a_send,
    a_recv,
):
    wide = lax.axis_index("wide")
    n = lax.axis_index("narrow")
    core = lax.rem(wide, CORES)
    z = rem4(lax.div(wide, CORES))
    y = rem4(lax.div(wide, CORES * Z))
    x = lax.div(wide, CORES * Z * Y)
    a = core * x + (1 - core) * y
    b = core * y + (1 - core) * x
    place = 16 * core + 4 * a + b
    column = x * Y + y
    flat = column * CORES + core
    height = n * Z + z

    def in_plane(step):
        to = lax.rem(flat + step, PLANE)
        to_column, to_core = lax.div(to, CORES), lax.rem(to, CORES)
        return to, to_column, to_core, (to_column * Z + z) * CORES + to_core

    def in_ring(step):
        to = lax.rem(height + step, Z * NARROW)
        to_n, to_z = lax.div(to, Z), lax.rem(to, Z)
        return to, to_n, to_z, (column * Z + to_z) * CORES + core

    def remote(src, dst, send_sem, recv_sem, to_wide, to_narrow):
        return pltpu.make_async_remote_copy(
            src_ref=src,
            dst_ref=dst,
            send_sem=send_sem,
            recv_sem=recv_sem,
            device_id={"wide": to_wide, "narrow": to_narrow},
            device_id_type=MESH,
        )

    def send(*what):
        copy = remote(*what)
        copy.start()
        return copy

    own = [
        pltpu.make_async_copy(draws_prev, d1.at[0], own_sem.at[0]),
        pltpu.make_async_copy(draws_panel, dv.at[0, 0], own_sem.at[1]),
        pltpu.make_async_copy(inverse, dv.at[1, 0], own_sem.at[2]),
        pltpu.make_async_copy(factor.at[pl.ds(128 * n, 128)], f_rows.at[0], own_sem.at[3]),
        pltpu.make_async_copy(corr.at[pl.ds(128 * n, 128)], c_rows.at[n], own_sem.at[4]),
    ]
    for copy in own:
        copy.start()

    barrier = pltpu.get_barrier_semaphore()

    def greet(to_wide, to_n):
        pl.semaphore_signal(
            barrier, inc=1, device_id={"wide": to_wide, "narrow": to_n}, device_id_type=MESH
        )

    turned = [[rem4(at + step) for step in range(4)] for at in (x, y, z, n)]
    for step in range(1, Z * NARROW):
        greet(wide_of(x, y, turned[2][step % 4], core), turned[3][step // 4])
    for step in range(1, PLANE):
        greet(
            wide_of(turned[0][step // 8], turned[1][step // 2 % 4], z, core if step % 2 == 0 else 1 - core), n
        )
    pl.semaphore_wait(barrier, Z * NARROW - 1 + PLANE - 1)
    for copy in own:
        copy.wait()

    rows8 = pl.ds(8 * place, 8)
    rows8_core = pl.ds(8 * (4 * a + b), 8)
    rows16 = pl.ds(16 * place, 16)
    quarter = pl.ds(pl.multiple_of(128 * z, 128), 128)
    d_copies = []
    for k in (2, 1, 3):
        for kind, ref in enumerate((d1.at[:, rows8, quarter], dv.at[core, :, rows8_core, quarter])):
            d_copies.append(
                send(
                    ref.at[0], ref.at[4 - k], d_send.at[k - 1, kind], d_recv.at[k - 1, kind], wide, rem4(n + k)
                )
            )

    def trade(k, kind):
        peer = rem4(n + k)
        if kind < 2:
            src = factor.at[pl.ds(128 * peer + 64 * kind, 64)]
            dst = f_rows.at[4 - k, pl.ds(64 * kind, 64)]
        else:
            src, dst = corr.at[pl.ds(128 * peer, 128)], c_rows.at[n]
        return remote(src, dst, f_send.at[k - 1, kind], f_recv.at[k - 1, kind], wide, peer)

    @pl.when(z != 1)
    def _():
        trade(2, 2).start()

    def to_plane(to):
        to_core, to_a, to_b = to // 16, (to // 4) % 4, to % 4
        to_x, to_y = (to_a, to_b) if to_core else (to_b, to_a)
        rows = pl.ds(16 * to, 16)
        return remote(
            factor.at[rows], piv.at[0, rows], p1_send, p1_recv, wide_of(to_x, to_y, 1, to_core), n
        )

    @pl.when(wide == OWNER)
    def _():
        for to in range(1, PLANE):
            to_plane(to).start()
        local = pltpu.make_async_copy(factor.at[pl.ds(0, 16)], piv.at[0, pl.ds(0, 16)], own_sem.at[0])
        local.start()
        local.wait()

    @pl.when((z == 1) & (wide != OWNER))
    def _():
        pltpu.make_async_copy(piv.at[0, rows16], piv.at[0, rows16], p1_recv).wait()

    def along_z(k, z_other):
        return remote(
            piv.at[0, rows16],
            piv.at[(4 - k) % 4, rows16],
            p2_send,
            p2_recv.at[(4 - k) % 4],
            wide_of(x, y, z_other, core),
            rem4(n + k),
        )

    others = [(k, z_other) for k in (2, 1, 3, 0) for z_other in range(Z) if (k, z_other) != (0, 1)]

    @pl.when(z == 1)
    def _():
        for k, z_other in others:
            along_z(k, z_other).start()
        trade(2, 2).start()

    def piece(kind, first, count):
        if kind == 0:
            return d1.at[pl.ds(1, 3), pl.ds(8 * first, 8 * count)]
        if kind == 1:
            return dv.at[core, pl.ds(1, 3), pl.ds(8 * (first - 16 * core), 8 * count)]
        return piv.at[:, pl.ds(16 * first, 16 * count)]

    def along(step, use_y):
        return wide_of(rem4(x + step * (1 - use_y)), rem4(y + step * use_y), z, core)

    def gather_first(kind):
        ref = piece(kind, place, 1)
        return [
            send(ref, ref, g1_send.at[step - 1, kind], g1_recv.at[step - 1, kind], along(step, core), n)
            for step in (1, 3, 2)
        ]

    partner = wide_of(x, y, z, 1 - core)

    def to_partner(kind, group, index):
        ref = piece(kind, 16 * core + 4 * group, 4)
        return send(ref, ref, x_send.at[index, kind], x_recv.at[index, kind], partner, n)

    def gather_second(kind):
        ref = piece(kind, 16 * core + 4 * a, 4)
        return {
            step: send(ref, ref, g2_send.at[step // 2, kind], g2_recv.at[step // 2, kind], along(step, 1 - core), n)
            for step in (1, 3)
        }

    def pass_on(kind, step):
        group, half = rem4(a + 4 - step), step // 2
        ref = piece(kind, 16 * core + 4 * group + 2 * half, 2)
        return send(ref, ref, g3_send.at[half, kind], g3_recv.at[half, kind], along(step, 1 - core), n)

    for copy in d_copies:
        copy.wait_recv()
    z_copies = []
    for step in (1, 2, 3):
        to_wide = wide_of(x, y, rem4(z + step), core)
        for kind, ref in enumerate((d1.at[pl.ds(1, 3), rows8, quarter], dv.at[core, pl.ds(1, 3), rows8_core, quarter])):
            z_copies.append(send(ref, ref, z_send.at[step - 1, kind], z_recv.at[step - 1, kind], to_wide, n))
    trade(1, 2).start()
    trade(3, 2).start()
    for copy in z_copies:
        copy.wait()
    first_d = [gather_first(0), gather_first(1)]
    for slot in range(1, NARROW):
        pltpu.make_async_copy(piv.at[slot, rows16], piv.at[slot, rows16], p2_recv.at[slot]).wait()

    @pl.when(z != 1)
    def _():
        pltpu.make_async_copy(piv.at[0, rows16], piv.at[0, rows16], p2_recv.at[0]).wait()

    f_copies = {(k, half): trade(k, half) for k in (2, 1, 3) for half in range(2)}
    c_copies = {k: trade(k, 2) for k in (2, 1, 3)}
    for half in range(2):
        for k in (2, 1, 3):
            f_copies[k, half].start()
    first_p = gather_first(2)

    second, core_copies = [], []
    for kind in (0, 1):
        for copy in first_d[kind]:
            copy.wait()
        second.append(gather_second(kind))
        core_copies.append(to_partner(kind, a, 0))
    for copy in first_p:
        copy.wait()
    second.append(gather_second(2))
    core_copies.append(to_partner(2, a, 0))
    third = []
    for kind in range(3):
        for step in (1, 3):
            second[kind][step].wait_recv()
            third.append(pass_on(kind, step))
            core_copies.append(to_partner(kind, rem4(a + 4 - step), step))
    for kind in range(3):
        third[2 * kind].wait_recv()
        third[2 * kind + 1].wait_recv()
        core_copies.append(to_partner(kind, rem4(a + 2), 2))
    for copy in d_copies:
        copy.wait_send()
    for copies in second:
        copies[1].wait_send()
        copies[3].wait_send()
    for copy in third:
        copy.wait_send()
    for copy in core_copies:
        copy.wait()

    @pl.when(wide == OWNER)
    def _():
        sent = piv.at[0, pl.ds(0, 16 * (PLANE - 1))]
        pltpu.make_async_copy(sent, sent, p1_send).wait()

    @pl.when(z == 1)
    def _():
        sent = piv.at[0, pl.ds(0, 16 * (Z * NARROW - 1))]
        pltpu.make_async_copy(sent, sent, p2_send).wait()

    for k in range(NARROW):
        piv_split[0, k], piv_split[1, k] = split(piv[k])
        d1_split[0, k], d1_split[1, k] = split(d1[k])
        for which in range(2):
            dv_split[0, which, k], dv_split[1, which, k] = split(dv[which, k])

    inverse_split = tuple(dv_split[part, 1].reshape(512, 512) for part in range(2))
    draws_split = tuple(dv_split[part, 0].reshape(512, 512) for part in range(2))
    q_copies = {
        (k, half): remote(
            panel.at[k, pl.ds(64 * half, 64)],
            panel_out.at[pl.ds(128 * n + 64 * half, 64)],
            q_send.at[k - 1, half],
            q_recv.at[k - 1, half],
            wide,
            rem4(n + k),
        )
        for k in (1, 2, 3)
        for half in range(2)
    }
    for half in range(2):
        rows = pl.ds(64 * half, 64)
        product = jnp.zeros((64, 512), jnp.float32)
        sums = jnp.zeros((64, 512), jnp.float32)
        squares = jnp.zeros((64, 1), jnp.float32)
        for k in (0, 1, 3, 2):
            if k:
                f_copies[4 - k, half].wait_recv()
            if half and k == 2:
                q_copies[2, 0].start()
            part = f_rows[k, rows]
            squares = squares + jnp.sum(part * part, axis=1, keepdims=True)
            part = split(part)
            product = product + dot3(part, (piv_split[0, k], piv_split[1, k]), 1, 1)
            sums = sums + dot3(part, (d1_split[0, k], d1_split[1, k]), 1, 0)
        if half == 0:
            for k in (1, 3, 2):
                c_copies[k].wait_recv()
        for m in range(NARROW):
            updated[:, 128 * m : 128 * m + 128] = c_rows[m, rows] - product[:, 128 * m : 128 * m + 128]
        value = dot3(split(updated[...]), inverse_split, 1, 1)
        for k in range(NARROW):
            panel[k, rows] = value[:, 128 * k : 128 * k + 128]
        squares = squares + jnp.sum(value * value, axis=1, keepdims=True)
        sums = sums + dot3(split(value), draws_split, 1, 0)
        scaled = sums * lax.rsqrt(squares + 1e-06)
        flat_uni[rows, :] = 0.5 * (1.0 + lax.erf(scaled * HALF_ROOT))
    for m in range(NARROW):
        uni[m] = flat_uni[:, 128 * m : 128 * m + 128].T.reshape(X * Y, Z, CORES, 1, 128)

    def up(step, carry):
        to, to_n, to_z, to_wide = in_ring(lax.rem(7 * step, Z * NARROW))
        remote(
            uni.at[to_n, :, to_z], mixed.at[:, :, z, n], u_send, u_recv, to_wide, to_n
        ).start()
        return carry

    lax.fori_loop(1, Z * NARROW, up, 0)
    local = pltpu.make_async_copy(uni.at[n, :, z], mixed.at[:, :, z, n], own_sem.at[0])
    local.start()
    kept = pltpu.make_async_copy(panel.at[0], panel_out.at[pl.ds(128 * n, 128)], own_sem.at[2])
    kept.start()
    local.wait()

    moved = mixed.at[pl.ds(0, Z * NARROW - 1)]
    pltpu.make_async_copy(moved, moved, u_recv).wait()
    pltpu.make_async_copy(moved, moved, u_send).wait()

    def hand_out(step, carry):
        to, to_column, to_core, to_wide = in_plane(step)
        remote(
            mixed.at[to_column, to_core], full.at[column, :, core], a_send, a_recv, to_wide, n
        ).start()
        return carry

    lax.fori_loop(1, PLANE, hand_out, 0)
    q_copies[2, 1].start()
    for half in range(2):
        for k in (1, 3):
            q_copies[k, half].start()
    local = pltpu.make_async_copy(mixed.at[column, core], full.at[column, :, core], own_sem.at[1])
    local.start()
    local.wait()

    moved = piv.at[0, pl.ds(0, 8 * (PLANE - 1))]
    pltpu.make_async_copy(moved, moved, a_recv).wait()
    pltpu.make_async_copy(moved, moved, a_send).wait()

    now = full[...].reshape(512, 128)
    row = lax.broadcasted_iota(jnp.int32, (512, 128), 0)
    lane = lax.broadcasted_iota(jnp.int32, (512, 128), 1)
    before = jnp.where(row == 0, 0.0, pltpu.roll(now, 1, 0))
    after = jnp.where(row == 511, 0.0, pltpu.roll(now, 511, 0))
    total = 6.0 / 16.0 * now
    for shift, weight in ((1, 4.0 / 16.0), (2, 1.0 / 16.0)):
        left = jnp.where(lane < shift, pltpu.roll(before, shift, 1), pltpu.roll(now, shift, 1))
        right = jnp.where(lane >= 128 - shift, pltpu.roll(after, 128 - shift, 1), pltpu.roll(now, 128 - shift, 1))
        total = total + weight * (left + right)
    smooth_out[...] = total
    for copy in (*f_copies.values(), *c_copies.values()):
        copy.wait_send()
    for copy in q_copies.values():
        copy.wait()
    kept.wait()


def per_device(corr_panel, factor_prev, draws_prev, draws_panel, diag_inverse):
    anywhere = pl.BlockSpec(memory_space=pl.ANY)
    dma = pltpu.SemaphoreType.DMA
    panel_factor, smoothed = pl.pallas_call(
        kernel,
        name="panel",
        out_shape=(
            jax.ShapeDtypeStruct((512, 128), jnp.float32),
            jax.ShapeDtypeStruct((512, 128), jnp.float32),
        ),
        in_specs=[anywhere] * 5,
        out_specs=(pl.BlockSpec(memory_space=pltpu.VMEM), pl.BlockSpec(memory_space=pltpu.VMEM)),
        scratch_shapes=[
            pltpu.VMEM((4, 128, 256), jnp.float32),
            pltpu.VMEM((4, 128, 128), jnp.float32),
            pltpu.VMEM((4, 256, 512), jnp.float32),
            pltpu.VMEM((2, 4, 128, 512), jnp.float32),
            pltpu.VMEM((4, 512, 256), jnp.float32),
            pltpu.VMEM((2, 4, 256, 512), jnp.bfloat16),
            pltpu.VMEM((2, 2, 4, 128, 512), jnp.bfloat16),
            pltpu.VMEM((2, 4, 512, 256), jnp.bfloat16),
            pltpu.VMEM((64, 512), jnp.float32),
            pltpu.VMEM((128, 512), jnp.float32),
            pltpu.VMEM((4, 128, 128), jnp.float32),
            pltpu.VMEM((4, X * Y, Z, CORES, 1, 128), jnp.float32),
            pltpu.VMEM((X * Y, CORES, Z, NARROW, 1, 128), jnp.float32),
            pltpu.VMEM((X * Y, Z, CORES, NARROW, 1, 128), jnp.float32),
            pltpu.VMEM((512, 128), jnp.float32),
            dma((5,)),
            dma((3, 2)),
            dma((3, 2)),
            dma((3, 2)),
            dma((3, 2)),
            dma,
            dma,
            dma,
            dma((4,)),
            dma((3, 3)),
            dma((3, 3)),
            dma((3, 3)),
            dma((3, 3)),
            dma((2, 3)),
            dma((2, 3)),
            dma((2, 3)),
            dma((2, 3)),
            dma((4, 3)),
            dma((4, 3)),
            dma((3, 2)),
            dma((3, 2)),
            dma,
            dma,
            dma,
            dma,
        ],
        compiler_params=pltpu.CompilerParams(
            collective_id=0, has_side_effects=True, vmem_limit_bytes=40 * 2**20
        ),
    )(*(pltpu.with_memory_space_constraint(v, pltpu.HBM) for v in (corr_panel, factor_prev, draws_prev, draws_panel, diag_inverse)))
    return panel_factor, smoothed.reshape(1, 512 * 128)


def solution(mesh):
    in_specs = (
        P("wide", "narrow"),
        P("wide", "narrow"),
        P("narrow", None),
        P("narrow", None),
        P("narrow", None),
    )
    out_specs = (P("wide", "narrow"), P(("narrow", "wide"), None))
    return jax.shard_map(
        per_device, mesh=mesh, in_specs=in_specs, out_specs=out_specs, check_vma=False
    )
```
